32 devices in a mesh: groups: 2 (over y), tmpl: 4 (over z), sta: 2 (over x), comp: 2 (over core).
Axes of the slice: x: 2, y: 2, z: 4, core: 2. Of those that a mesh axis runs over, the one named last changes fastest.
Arguments:
- templates: bfloat16 [1024, 32, 3, 256], P(('groups', 'tmpl'), ('sta', 'comp')), parts along dimension 0, may hold values from -6 to 6
- data: bfloat16 [64, 3, 2048], P(('groups', 'sta', 'comp'), None, 'tmpl'), parts along dimension 0, may hold values from -21 to 21
- tail: bfloat16 [64, 3, 512], P(('groups', 'sta', 'comp')), parts along dimension 0, may hold values from -21 to 21
- offsets: int32 [64], P(('groups', 'sta', 'comp')), parts along dimension 0, may hold values from 0 to 255, as said below
- weights: int32 [64], P(('groups', 'sta', 'comp')), parts along dimension 0, may hold values from 1 to 4
- mask: int32 [1024, 32], P(('groups', 'tmpl'), ('sta', 'comp')), parts along dimension 0, may hold values 0 or 1
Outputs:
- stack: float32 [1024, 2048], P(('groups', 'tmpl'), ('sta', 'comp')), parts along dimension 0
The draws below stay inside these ranges and needn't reach their ends.
There are 2 independent parts, one for each index of `groups`. The reference program is written for one: setup_inputs(seed, part) draws one part's arguments, and reference() takes and returns one part's arrays. A program takes and returns all parts, laid end to end along the dimension named above; each array names one. Nothing has to cross between parts.
Inputs may be any that keep to these rules, and one draw needn't show every extreme that they name: `offsets`: some station's offset is 0 and some station's is 255.
All inputs are finite; a program needn't handle non-finite values. No bound on the sum of `mask` on one device may be relied on, other than what follows from the above.
Results may differ from the reference program's by a relative error of at most 0.0055.
Values may be sent and summed in bfloat16 or wider, within the bound.
No kernel may reach another device: no remote copies, remote signals or barrier semaphores. Data moves between devices by JAX's collectives and lax.ppermute only.
A program may use at most 192 MiB of HBM per device.

```python
import jax
import jax.numpy as jnp
from jax import lax

TEMPLATES = 512
L = 256
STATIONS = 32
NLAG = 2048


def trace_levels(key):
    amplitude = jnp.exp(jax.random.uniform(jax.random.fold_in(key, 11), (STATIONS, 3, 1), jnp.float32, jnp.log(0.3), jnp.log(3.0)))
    level = jax.random.uniform(jax.random.fold_in(key, 12), (STATIONS, 3, 1), jnp.float32, -2.0, 2.0)
    return (amplitude, level)


def draw_data(key, part):
    amplitude, level = trace_levels(key)
    noise_key = jax.random.fold_in(key, 13)
    noise = jnp.clip(jax.random.normal(noise_key, (STATIONS, 3, NLAG), jnp.float32), -5.0, 5.0)
    return (amplitude * (noise + level)).astype(jnp.bfloat16)


def draw_tail(key, part):
    amplitude, level = trace_levels(key)
    noise_key = jax.random.fold_in(key, 14)
    noise = jnp.clip(jax.random.normal(noise_key, (STATIONS, 3, 2 * L), jnp.float32), -5.0, 5.0)
    return (amplitude * (noise + level)).astype(jnp.bfloat16)


def draw_offsets(key, part):
    initial = jax.random.randint(jax.random.fold_in(key, 21), (STATIONS,), 0, L)
    highest = jax.random.randint(jax.random.fold_in(key, 22), (), 0, STATIONS)
    stride = jax.random.randint(jax.random.fold_in(key, 23), (), 1, STATIONS)
    lowest = (highest + stride) % STATIONS
    places = jnp.arange(STATIONS)
    initial = jnp.where(places == highest, L - 1, initial)
    initial = jnp.where(places == lowest, 0, initial)
    return initial.astype(jnp.int32)


def touch_ends(drawn, stream_key, smallest, largest):
    place = [jax.random.randint(jax.random.fold_in(stream_key, axis), (), 0, length) for axis, length in enumerate(drawn.shape)]
    widest = drawn.shape.index(max(drawn.shape))
    neighbour = place[:widest] + [(place[widest] + 1) % drawn.shape[widest]] + place[widest + 1:]
    return drawn.at[tuple(place)].set(smallest).at[tuple(neighbour)].set(largest)


def level_of(rng, extent, cuts, least, high):
    def one(axis_at, shards_of):
        heights = jax.random.uniform(jax.random.fold_in(jax.random.fold_in(rng, 6), axis_at), (shards_of,), jnp.float32, least / len(cuts), high / len(cuts))
        return jnp.repeat(jnp.exp(heights), extent[axis_at] // shards_of).reshape((-1,) + (1,) * (len(extent) - axis_at - 1))

    factor_of = one(*cuts[0])
    for cut in cuts[1:]:
        factor_of = factor_of * one(*cut)
    return factor_of


def gaussian(key, extent, deviation, reach, pieces=(), held_as=jnp.bfloat16):
    loudness = level_of(key, extent, pieces, -0.22, 0.18) if pieces else 1.0
    entries = jax.random.normal(key, extent, jnp.float32) * deviation * loudness
    return jnp.minimum(jnp.maximum(entries, -reach), reach).astype(held_as)


def setup_inputs(seed: int = 0, part: int = 0) -> dict:
    streams_of = jax.random.split(jax.random.key(seed), 7)
    part_splits = jax.random.split(jax.random.fold_in(streams_of[6], part), 7)
    templates = gaussian(part_splits[0], (TEMPLATES, STATIONS, 3, L), 1.0, 6.0, ((0, 4), (1, 4)))
    data = draw_data(jax.random.fold_in(jax.random.fold_in(streams_of[6], part), 71), part)
    tail = draw_tail(jax.random.fold_in(jax.random.fold_in(streams_of[6], part), 71), part)
    offsets = draw_offsets(jax.random.fold_in(jax.random.fold_in(streams_of[6], part), 71), part)
    weights = touch_ends(jax.random.randint(part_splits[4], (STATIONS,), 1, 5), jax.random.fold_in(part_splits[4], 1), 1, 4).astype(jnp.int32)
    mask = touch_ends((jax.random.randint(part_splits[5], (TEMPLATES, STATIONS), 0, 4) < 3).astype(jnp.int32), jax.random.fold_in(part_splits[5], 1), 0, 1)
    return {"templates": templates, "data": data, "tail": tail, "offsets": offsets, "weights": weights, "mask": mask}


EPS = 1e-05

def unit_templates(templates):
    values = templates.astype(jnp.float32)
    centred = values - lax.optimization_barrier(jnp.mean(values, axis=-1, keepdims=True))
    spread = lax.optimization_barrier(jnp.mean(centred * centred, axis=-1, keepdims=True))
    return (centred * lax.rsqrt(spread + EPS)).astype(jnp.bfloat16)

def window_factor(values, length):
    shape_ones = (1,) * (values.ndim - 1)
    anchor = jnp.zeros((), values.dtype)
    sums = lax.reduce_window(values, anchor, lax.add, shape_ones + (length,), shape_ones + (1,), 'VALID')
    squares = lax.reduce_window(values * values, anchor, lax.add, shape_ones + (length,), shape_ones + (1,), 'VALID')
    middle = sums / length
    spread = squares / length - middle * middle
    return 1.0 / (length * jnp.sqrt(spread + EPS))

def reference(templates, data, tail, offsets, weights, mask):
    units = unit_templates(templates)
    whole = jnp.concatenate([data, tail], axis=2)
    station_weight = mask.astype(jnp.float32) * weights.astype(jnp.float32)[None, :]
    lag_index = jnp.arange(L, dtype=jnp.int32)[:, None] + jnp.arange(NLAG, dtype=jnp.int32)[None, :]

    def one_station(total, inputs):
        unit_rows, trace, begin, column = inputs
        window = lax.dynamic_slice_in_dim(trace, begin.astype(jnp.int32), NLAG + L - 1, 1).astype(jnp.float32)
        factor = window_factor(window, L)
        for component in range(3):
            hankel = window[component][lag_index]
            products = jnp.dot(unit_rows[:, component].astype(jnp.float32), hankel, precision=lax.Precision.HIGHEST, preferred_element_type=jnp.float32)
            total = total + column[:, None] * products * factor[component][None, :]
        return (total, None)
    start_total = jnp.zeros((TEMPLATES, NLAG), jnp.float32)
    stacked, _ = lax.scan(one_station, start_total, (jnp.transpose(units, (1, 0, 2, 3)), whole, offsets, jnp.transpose(station_weight)))
    return stacked
```

```python
import functools

import jax
import jax.numpy as jnp
from jax import lax
from jax.experimental import pallas as pl
from jax.experimental.pallas import tpu as pltpu
from jax.sharding import PartitionSpec as P

EPS = 1e-05
S = 4
LANES = 128
VMEM = pl.BlockSpec(memory_space=pltpu.VMEM)
SMEM = pl.BlockSpec(memory_space=pltpu.SMEM)
PIECES = (((0, 0), (1, 0)), ((2, 0), (3, 0)), ((2, 1), (3, 1)), ((3, 1), (0, 0)), ((1, 0), (2, 0)), ((1, 1), (2, 1)))
PHASE_COLUMNS = ((0, 1), (3, 4), (2, 0), (5, 3))


def iota(shape, axis):
    return lax.broadcasted_iota(jnp.int32, shape, axis)


def template_kernel(x_ref, mask_ref, wide_ref, last_ref, unit_ref, rows_ref):
    count, comps, stations, length = x_ref.shape
    pairs = comps * stations
    group = 8
    for at in range(0, count, group):
        values = x_ref[at : at + group].astype(jnp.float32).reshape(group * pairs, length)
        centred = values - jnp.sum(values, axis=-1, keepdims=True) * (1.0 / length)
        spread = jnp.sum(centred * centred, axis=-1, keepdims=True) * (1.0 / length)
        unit = centred * lax.rsqrt(spread + EPS)
        for h in range(length // LANES):
            unit_ref[h, at * pairs : (at + group) * pairs, :] = unit[:, LANES * h : LANES * (h + 1)]
    available = jnp.transpose(mask_ref[...].astype(jnp.float32))
    for s in range(stations):
        column = available[:, s : s + 1]
        for c in range(comps):
            pair = c * stations + s
            rows = jnp.concatenate(
                [unit_ref[h, pl.ds(pair, count, stride=pairs), :] for h in range(length // LANES)], axis=1
            )
            rows_ref[pair * count : (pair + 1) * count, :] = (rows * column).astype(jnp.bfloat16)
    group_rows = length // S
    sample = iota((length, LANES), 0)
    lane = iota((length, LANES), 1)
    place = lane % group_rows
    first = lane < group_rows
    lane_row = iota((count, LANES), 1)
    last = jnp.zeros((count, LANES), jnp.float32)
    wanted = []
    for low, high in PIECES:
        base = jnp.where(first, low[0] - S * low[1], high[0] - S * high[1])
        wanted.append(jnp.where(sample == S * (group_rows - 1 - place) + base, 1.0, 0.0).astype(jnp.bfloat16))
    batch = 8
    for at in range(0, pairs, batch):
        span = rows_ref[at * count : (at + batch) * count, :]
        for v in range(0, len(PIECES), 2):
            moved = jnp.dot(span, jnp.concatenate(wanted[v : v + 2], axis=1), preferred_element_type=jnp.float32)
            for i in range(batch):
                part = moved[i * count : (i + 1) * count]
                wide_ref[at + i, :, LANES * v : LANES * v + 2 * LANES] = part.astype(jnp.bfloat16)
                pair = at + i
                if v == 0:
                    turned = pltpu.roll(part[:, LANES:], (pair - 32) % LANES, axis=1)
                    last = jnp.where(lane_row == 32 + pair, turned, last)
                if v == 4:
                    turned = pltpu.roll(part[:, :LANES], pair, axis=1)
                    last = jnp.where((lane_row == pair) | (lane_row == 64 + pair), turned, last)
    last_ref[...] = last.astype(jnp.bfloat16)


def templates_prepared(templates, mask):
    count, stations, comps, length = templates.shape
    pairs = stations * comps
    return pl.pallas_call(
        template_kernel,
        out_shape=(
            jax.ShapeDtypeStruct((pairs, count, LANES * len(PIECES)), jnp.bfloat16),
            jax.ShapeDtypeStruct((count, LANES), jnp.bfloat16),
        ),
        in_specs=[VMEM, VMEM],
        out_specs=(VMEM, VMEM),
        scratch_shapes=[
            pltpu.VMEM((length // LANES, pairs * count, LANES), jnp.float32),
            pltpu.VMEM((pairs * count, length), jnp.bfloat16),
        ],
        compiler_params=pltpu.CompilerParams(vmem_limit_bytes=24 << 20),
        cost_estimate=pl.CostEstimate(flops=2 * 10**9, bytes_accessed=8 * 10**6, transcendentals=0),
        name="templates",
    )(jnp.transpose(templates, (0, 2, 1, 3)), jnp.transpose(mask))


def later(x, by):
    return pltpu.roll(x, x.shape[-1] - by, axis=1)


def data_kernel(blocks, scal_ref, offsets_ref, weights_ref, *refs):
    block_refs, (phases_ref, ahead_ref, factor_ref, raw_ref) = refs[: blocks + 1], refs[blocks + 1 :]
    comps, stations, width = block_refs[0].shape
    pairs = comps * stations
    unitw = S * LANES
    per = width // unitw
    for i in range(blocks + 1):
        values = block_refs[i][...].astype(jnp.float32).reshape(pairs, block_refs[i].shape[-1])
        home = blocks if i == blocks else lax.rem(scal_ref[0] + i, blocks)
        for j in range(block_refs[i].shape[-1] // unitw):
            raw_ref[home * per + j] = values[:, unitw * j : unitw * (j + 1)]
    parts = raw_ref.shape[0]
    sample = iota((unitw, unitw), 0)
    lane = iota((unitw, unitw), 1)
    pick = jnp.where(sample == S * (lane % LANES) + lane // LANES, 1.0, 0.0).astype(jnp.bfloat16)
    flat = raw_ref[...].reshape(parts * pairs, unitw).astype(jnp.bfloat16)
    split = jnp.dot(flat, pick, preferred_element_type=jnp.float32)
    full = parts * LANES
    row = iota((stations, full), 0)
    offset = jnp.zeros((stations, full), jnp.int32)
    weight = jnp.zeros((stations, full), jnp.float32)
    for s in range(stations):
        offset = jnp.where(row == s, offsets_ref[s], offset)
        weight = jnp.where(row == s, weights_ref[s].astype(jnp.float32), weight)
    length = 256
    group_rows = length // S
    for c in range(comps):
        at = c * stations
        v = [
            jnp.concatenate(
                [split[b * pairs + at : b * pairs + at + stations, LANES * p : LANES * (p + 1)] for b in range(parts)], axis=1
            )
            for p in range(S)
        ]
        step = 1
        while S * step < length:
            taken = (offset & (S * step)) != 0
            v = [jnp.where(taken, later(x, step), x) for x in v]
            step *= 2
        for bit in (2, 1):
            taken = (offset & bit) != 0
            v = [jnp.where(taken, v[p + bit] if p + bit < S else later(v[p + bit - S], 1), v[p]) for p in range(S)]
        ahead = [later(x, group_rows) for x in v]
        mean = v[0] + v[1] + v[2] + v[3]
        power = v[0] * v[0] + v[1] * v[1] + v[2] * v[2] + v[3] * v[3]
        step = 1
        while step < group_rows:
            mean = mean + later(mean, step)
            power = power + later(power, step)
            step *= 2
        for r in range(S):
            middle = mean * (1.0 / length)
            spread = power * (1.0 / length) - middle * middle
            factor_ref[r, at : at + stations, :] = weight / (length * jnp.sqrt(spread + EPS))
            if r + 1 < S:
                mean = mean + (ahead[r] - v[r])
                power = power + (ahead[r] * ahead[r] - v[r] * v[r])
                ahead_ref[r, at : at + stations, :] = ahead[r]
            phases_ref[r, at : at + stations, :] = v[r]


def data_prepared(place, offsets, weights, blocks, tail):
    comps, stations, width = blocks[0].shape
    pairs = comps * stations
    unitw = S * LANES
    parts = (len(blocks) * width + tail.shape[-1]) // unitw
    full = parts * LANES
    return pl.pallas_call(
        functools.partial(data_kernel, len(blocks)),
        out_shape=(
            jax.ShapeDtypeStruct((S, pairs, full), jnp.float32),
            jax.ShapeDtypeStruct((S - 1, pairs, full), jnp.float32),
            jax.ShapeDtypeStruct((S, pairs, full), jnp.float32),
        ),
        in_specs=[SMEM, SMEM, SMEM] + [VMEM] * (len(blocks) + 1),
        out_specs=(VMEM, VMEM, VMEM),
        scratch_shapes=[pltpu.VMEM((parts, pairs, unitw), jnp.float32)],
        compiler_params=pltpu.CompilerParams(vmem_limit_bytes=24 << 20),
        cost_estimate=pl.CostEstimate(flops=10**9, bytes_accessed=2 * 10**6, transcendentals=0),
        name="records",
    )(place, offsets, weights, *blocks, tail)


def chunk_kernel(lags, scal_ref, wide_ref, last_ref, phases_ref, ahead_ref, factor_ref, away_ref, keep_ref, sum_ref):
    pairs, count, _ = wide_ref.shape
    group_rows = 64
    half = lags // S // 2
    chunk, mine = scal_ref[0], scal_ref[1]
    start = pl.multiple_of(chunk * (lags // S), LANES)
    lane = iota((8, LANES), 1)
    sub = iota((8, LANES), 0)
    tile = 2 * LANES
    for n in range(lags // S // tile):
        begin = start + n * tile
        begin = pl.multiple_of(begin, LANES)

        def factor_of(r, row):
            return factor_ref[r, row, pl.ds(begin, tile)]

        extra = []
        for r in range(S):
            held = {}
            for i in range(3):
                j = i - (3 - r)
                if j >= 0:
                    scaled = ahead_ref[j, :, pl.ds(begin, tile)] * factor_ref[r, :, pl.ds(begin, tile)]
                    held[i] = jnp.concatenate([scaled, jnp.zeros((32 - pairs, tile), jnp.float32)], axis=0)
            if held:
                none = jnp.zeros((32, tile), jnp.float32)
                table = jnp.concatenate([held.get(0, none), held.get(2, none), held.get(1, none), none], axis=0)
                extra.append(jnp.dot(last_ref[...], table.astype(jnp.bfloat16), preferred_element_type=jnp.float32))
            else:
                extra.append(None)
        for pair in range(pairs):
            rows = []
            for p in range(S):
                line = [
                    jnp.broadcast_to(phases_ref[p, pair : pair + 1, pl.ds(begin + LANES * j, LANES)], (8, LANES))
                    for j in range(3)
                ]
                for g in range(0, group_rows, 16):
                    sides = []
                    for j in range(2):
                        pieces = []
                        for h in (g, g + 8):
                            ahead = group_rows - 1 - h - sub
                            mixed = jnp.where(lane >= ahead, line[j], line[j + 1])
                            pieces.append(
                                pltpu.roll(mixed, LANES - (group_rows - 1) + h, axis=1, stride=1, stride_axis=0)
                            )
                        sides.append(jnp.concatenate(pieces, axis=0).astype(jnp.bfloat16))
                    rows.append(jnp.concatenate(sides, axis=1))
            table = jnp.concatenate(rows, axis=0)
            units = jnp.concatenate(
                [
                    jnp.concatenate([wide_ref[pair, :, LANES * v : LANES * (v + 1)] for v in PHASE_COLUMNS[r]], axis=1)
                    for r in range(S)
                ],
                axis=0,
            )
            products = jnp.dot(units, table, preferred_element_type=jnp.float32)
            for r in range(S):
                factor = factor_ref[r, pair : pair + 1, pl.ds(begin, tile)]
                scaled = products[r * count : (r + 1) * count] * factor
                where = (slice(r * count, (r + 1) * count), slice(n * tile, (n + 1) * tile))
                if pair == 0:
                    sum_ref[where] = scaled if extra[r] is None else scaled + extra[r]
                else:
                    sum_ref[where] += scaled
    other = pl.multiple_of((1 - mine) * half, LANES)
    own = pl.multiple_of(mine * half, LANES)
    for r in range(S):
        away_ref[:, r * half : (r + 1) * half] = sum_ref[r * count : (r + 1) * count, pl.ds(other, half)].astype(jnp.bfloat16)
        keep_ref[:, r * half : (r + 1) * half] = sum_ref[r * count : (r + 1) * count, pl.ds(own, half)]


def chunk_sum(lags, chunk, mine, wide, last, phases, ahead, factor):
    pairs, count, _ = wide.shape
    return pl.pallas_call(
        functools.partial(chunk_kernel, lags),
        out_shape=(
            jax.ShapeDtypeStruct((count, lags // 2), jnp.bfloat16),
            jax.ShapeDtypeStruct((count, lags // 2), jnp.float32),
        ),
        in_specs=[SMEM] + [VMEM] * 5,
        out_specs=(VMEM, VMEM),
        scratch_shapes=[pltpu.VMEM((S * count, lags // S), jnp.float32)],
        compiler_params=pltpu.CompilerParams(vmem_limit_bytes=24 << 20),
        cost_estimate=pl.CostEstimate(
            flops=2 * count * pairs * 256 * lags, bytes_accessed=8 * 10**6, transcendentals=0
        ),
        name="chunk",
    )(jnp.stack([chunk, mine]).astype(jnp.int32), wide, last, phases, ahead, factor)


def finish_kernel(take, *refs):
    terms, out_ref = refs[:-1], refs[-1]
    total = terms[0][...].astype(jnp.float32)
    for term in terms[1:]:
        total = total + term[...].astype(jnp.float32)
    width = total.shape[-1]
    half = width // S
    lane = iota((width, width), 1)
    sample = iota((width, width), 0)
    pick = jnp.where(sample == (lane % S) * half + lane // S, 1.0, 0.0).astype(jnp.bfloat16)
    left = total
    result = None
    for _ in range(take):
        piece = left.astype(jnp.bfloat16)
        moved = jnp.dot(piece, pick, preferred_element_type=jnp.float32)
        result = moved if result is None else result + moved
        left = left - piece.astype(jnp.float32)
    out_ref[...] = result


def finished(*terms):
    return pl.pallas_call(
        functools.partial(finish_kernel, 2),
        out_shape=jax.ShapeDtypeStruct(terms[0].shape, jnp.float32),
        in_specs=[VMEM] * len(terms),
        out_specs=VMEM,
        compiler_params=pltpu.CompilerParams(vmem_limit_bytes=24 << 20),
        name="finish",
    )(*terms)


def shards(templates, data, tail, offsets, weights, mask):
    owners = lax.axis_size("tmpl")
    sides = lax.axis_size("sta")
    span = data.shape[-1]
    lags = owners * span // sides
    place = lax.axis_index("tmpl")
    side = lax.axis_index("sta")
    core = lax.axis_index("comp")
    block = jnp.transpose(data, (1, 0, 2))
    closing = jnp.transpose(tail, (1, 0, 2))
    if owners <= 4:
        blocks = [block] + [
            lax.ppermute(block, "tmpl", [(i, (i - d) % owners) for i in range(owners)]) for d in range(1, owners)
        ]
    else:
        gathered = lax.all_gather(block, "tmpl", axis=0, tiled=False)
        blocks = [lax.dynamic_index_in_dim(gathered, lax.rem(place + d, owners), 0, False) for d in range(owners)]
    wide, last = templates_prepared(templates, mask)
    phases, ahead, factor = data_prepared(place.reshape(1).astype(jnp.int32), offsets, weights, blocks, closing)
    terms = []
    for d in range(1, sides + 1):
        chunk = lax.rem(side + d, sides)
        away, keep = chunk_sum(lags, chunk, core, wide, last, phases, ahead, factor)
        got = lax.ppermute(away, "comp", [(0, 1), (1, 0)])
        if d < sides:
            both = (keep + got.astype(jnp.float32)).astype(jnp.bfloat16)
            terms.append(lax.ppermute(both, "sta", [(i, (i + d) % sides) for i in range(sides)]))
        else:
            terms += [keep, got]
    return finished(*terms)


def solution(mesh):
    in_specs = (
        P(("groups", "tmpl"), ("sta", "comp"), None, None),
        P(("groups", "sta", "comp"), None, "tmpl"),
        P(("groups", "sta", "comp"), None, None),
        P(("groups", "sta", "comp")),
        P(("groups", "sta", "comp")),
        P(("groups", "tmpl"), ("sta", "comp")),
    )
    out_specs = P(("groups", "tmpl"), ("sta", "comp"))
    return jax.shard_map(shards, mesh=mesh, in_specs=in_specs, out_specs=out_specs, check_vma=False)
```

```python
import functools

import jax
import jax.numpy as jnp
from jax import lax
from jax.experimental import pallas as pl
from jax.experimental.pallas import tpu as pltpu
from jax.sharding import PartitionSpec as P

EPS = 1e-05
BATCH = 3
S = 4
LANES = 128
VMEM = pl.BlockSpec(memory_space=pltpu.VMEM)
HBM = pl.BlockSpec(memory_space=pltpu.HBM)
SMEM = pl.BlockSpec(memory_space=pltpu.SMEM)
PIECES = (((0, 0), (1, 0)), ((2, 0), (3, 0)), ((2, 1), (3, 1)), ((3, 1), (0, 0)), ((1, 0), (2, 0)), ((1, 1), (2, 1)))
PHASE_COLUMNS = ((0, 1), (3, 4), (2, 0), (5, 3))


def iota(shape, axis):
    return lax.broadcasted_iota(jnp.int32, shape, axis)


def template_kernel(source_ref, mask_ref, wide_ref, last_ref, x_ref, unit_ref, rows_ref, held_ref, flag_ref, arrived, sent):
    count, comps, stations, length = x_ref.shape
    pairs = comps * stations
    group = 8
    quarter = count // 4
    copies = [
        pltpu.make_async_copy(
            source_ref.at[i * quarter : (i + 1) * quarter], x_ref.at[i * quarter : (i + 1) * quarter], arrived.at[i]
        )
        for i in range(4)
    ]
    flags = pltpu.make_async_copy(mask_ref, flag_ref, arrived.at[4])
    for copy in copies + [flags]:
        copy.start()
    for at in range(0, count, group):
        if at % quarter == 0:
            copies[at // quarter].wait()
        values = x_ref[at : at + group].astype(jnp.float32).reshape(group * pairs, length)
        centred = values - jnp.sum(values, axis=-1, keepdims=True) * (1.0 / length)
        spread = jnp.sum(centred * centred, axis=-1, keepdims=True) * (1.0 / length)
        unit = centred * lax.rsqrt(spread + EPS)
        for h in range(length // LANES):
            unit_ref[h, at * pairs : (at + group) * pairs, :] = unit[:, LANES * h : LANES * (h + 1)]
    flags.wait()
    available = jnp.transpose(flag_ref[...].astype(jnp.float32))
    for s in range(stations):
        column = available[:, s : s + 1]
        for c in range(comps):
            pair = c * stations + s
            rows = jnp.concatenate(
                [unit_ref[h, pl.ds(pair, count, stride=pairs), :] for h in range(length // LANES)], axis=1
            )
            rows_ref[pair * count : (pair + 1) * count, :] = (rows * column).astype(jnp.bfloat16)
    group_rows = length // S
    sample = iota((length, LANES), 0)
    lane = iota((length, LANES), 1)
    place = lane % group_rows
    first = lane < group_rows
    lane_row = iota((count, LANES), 1)
    last = jnp.zeros((count, LANES), jnp.float32)
    wanted = []
    for low, high in PIECES:
        base = jnp.where(first, low[0] - S * low[1], high[0] - S * high[1])
        wanted.append(jnp.where(sample == S * (group_rows - 1 - place) + base, 1.0, 0.0).astype(jnp.bfloat16))
    batch = 8
    leaving = []
    for at in range(0, pairs, batch):
        span = rows_ref[at * count : (at + batch) * count, :]
        for v in range(0, len(PIECES), 2):
            moved = jnp.dot(span, jnp.concatenate(wanted[v : v + 2], axis=1), preferred_element_type=jnp.float32)
            for i in range(batch):
                part = moved[i * count : (i + 1) * count]
                held_ref[at + i, :, LANES * v : LANES * v + 2 * LANES] = part.astype(jnp.bfloat16)
                pair = at + i
                if v == 0:
                    turned = pltpu.roll(part[:, LANES:], (pair - 32) % LANES, axis=1)
                    last = jnp.where(lane_row == 32 + pair, turned, last)
                if v == 4:
                    turned = pltpu.roll(part[:, :LANES], pair, axis=1)
                    last = jnp.where((lane_row == pair) | (lane_row == 64 + pair), turned, last)
        copy = pltpu.make_async_copy(held_ref.at[at : at + batch], wide_ref.at[at : at + batch], sent.at[at // batch])
        copy.start()
        leaving.append(copy)
    last_ref[...] = last.astype(jnp.bfloat16)
    for copy in leaving:
        copy.wait()


def in_hbm(x):
    return pltpu.with_memory_space_constraint(x, pltpu.HBM)


def templates_prepared(templates, mask):
    count, stations, comps, length = templates.shape
    pairs = stations * comps
    wide = (pairs, count, LANES * len(PIECES))
    wide, last = pl.pallas_call(
        template_kernel,
        out_shape=(pltpu.HBM(wide, jnp.bfloat16), jax.ShapeDtypeStruct((count, LANES), jnp.bfloat16)),
        in_specs=[HBM, HBM],
        out_specs=(HBM, VMEM),
        scratch_shapes=[
            pltpu.VMEM((count, comps, stations, length), jnp.bfloat16),
            pltpu.VMEM((length // LANES, pairs * count, LANES), jnp.float32),
            pltpu.VMEM((pairs * count, length), jnp.bfloat16),
            pltpu.VMEM(wide, jnp.bfloat16),
            pltpu.VMEM((stations, count), jnp.int32),
            pltpu.SemaphoreType.DMA((5,)),
            pltpu.SemaphoreType.DMA((pairs // 8,)),
        ],
        compiler_params=pltpu.CompilerParams(vmem_limit_bytes=24 << 20),
        cost_estimate=pl.CostEstimate(flops=2 * 10**9, bytes_accessed=8 * 10**6, transcendentals=0),
        name="templates",
    )(in_hbm(jnp.transpose(templates, (0, 2, 1, 3))), in_hbm(jnp.transpose(mask)))
    return wide, last


def later(x, by):
    return pltpu.roll(x, x.shape[-1] - by, axis=1)


def records(scal_ref, offsets_ref, weights_ref, block_refs, phases_ref, ahead_ref, factor_ref, raw_ref):
    blocks = len(block_refs) - 1
    comps, stations, width = block_refs[0].shape
    pairs = comps * stations
    unitw = S * LANES
    per = width // unitw
    for i in range(blocks + 1):
        values = block_refs[i][...].astype(jnp.float32).reshape(pairs, block_refs[i].shape[-1])
        home = blocks if i == blocks else lax.rem(scal_ref[0] + i, blocks)
        for j in range(block_refs[i].shape[-1] // unitw):
            raw_ref[home * per + j] = values[:, unitw * j : unitw * (j + 1)]
    parts = raw_ref.shape[0]
    column = iota((1, unitw), 1)
    pick = jnp.where(iota((unitw, unitw), 0) == S * (column % LANES) + column // LANES, 1.0, 0.0).astype(jnp.bfloat16)
    flat = raw_ref[...].reshape(parts * pairs, unitw).astype(jnp.bfloat16)
    split = jnp.dot(flat, pick, preferred_element_type=jnp.float32)
    full = parts * LANES
    row = iota((stations, full), 0)
    offset = jnp.zeros((stations, full), jnp.int32)
    weight = jnp.zeros((stations, full), jnp.float32)
    for s in range(stations):
        offset = jnp.where(row == s, offsets_ref[s], offset)
        weight = jnp.where(row == s, weights_ref[s].astype(jnp.float32), weight)
    length = 256
    group_rows = length // S
    for c in range(comps):
        at = c * stations
        v = [
            jnp.concatenate(
                [split[b * pairs + at : b * pairs + at + stations, LANES * p : LANES * (p + 1)] for b in range(parts)], axis=1
            )
            for p in range(S)
        ]
        step = 1
        while S * step < length:
            taken = (offset & (S * step)) != 0
            v = [jnp.where(taken, later(x, step), x) for x in v]
            step *= 2
        for bit in (2, 1):
            taken = (offset & bit) != 0
            v = [jnp.where(taken, v[p + bit] if p + bit < S else later(v[p + bit - S], 1), v[p]) for p in range(S)]
        ahead = [later(x, group_rows) for x in v]
        mean = v[0] + v[1] + v[2] + v[3]
        power = v[0] * v[0] + v[1] * v[1] + v[2] * v[2] + v[3] * v[3]
        step = 1
        while step < group_rows:
            mean = mean + later(mean, step)
            power = power + later(power, step)
            step *= 2
        for r in range(S):
            middle = mean * (1.0 / length)
            spread = power * (1.0 / length) - middle * middle
            factor_ref[r, at : at + stations, :] = weight / (length * jnp.sqrt(spread + EPS))
            if r + 1 < S:
                mean = mean + (ahead[r] - v[r])
                power = power + (ahead[r] * ahead[r] - v[r] * v[r])
                ahead_ref[r, at : at + stations, :] = ahead[r]
            phases_ref[r, at : at + stations, :] = v[r]


def chunk_sum(lags, precise, chunk, mine, arrivals, wide_ref, last_ref, phases_ref, ahead_ref, factor_ref, away_ref, keep_ref, sum_ref):
    pairs, count, _ = wide_ref.shape
    group_rows = 64
    half = lags // S // 2
    start = pl.multiple_of(chunk * (lags // S), LANES)
    lane = iota((8, LANES), 1)
    sub = iota((8, LANES), 0)
    tile = 2 * LANES
    for n in range(lags // S // tile):
        begin = start + n * tile
        begin = pl.multiple_of(begin, LANES)

        def factor_of(r, row):
            return factor_ref[r, row, pl.ds(begin, tile)]

        extra = []
        for r in range(S):
            held = {}
            for i in range(3):
                j = i - (3 - r)
                if j >= 0:
                    scaled = ahead_ref[j, :, pl.ds(begin, tile)] * factor_ref[r, :, pl.ds(begin, tile)]
                    held[i] = jnp.concatenate([scaled, jnp.zeros((32 - pairs, tile), jnp.float32)], axis=0)
            if held:
                none = jnp.zeros((32, tile), jnp.float32)
                table = jnp.concatenate([held.get(0, none), held.get(2, none), held.get(1, none), none], axis=0)
                extra.append(jnp.dot(last_ref[...], table.astype(jnp.bfloat16), preferred_element_type=jnp.float32))
            else:
                extra.append(None)
        for pair in range(pairs):
            if n == 0 and pair % BATCH == 0:
                arrivals[pair // BATCH].wait()
            rows = []
            for p in range(S):
                line = [
                    jnp.broadcast_to(phases_ref[p, pair : pair + 1, pl.ds(begin + LANES * j, LANES)], (8, LANES))
                    for j in range(3)
                ]
                for g in range(0, group_rows, 16):
                    sides = []
                    for j in range(2):
                        pieces = []
                        for h in (g, g + 8):
                            ahead = group_rows - 1 - h - sub
                            mixed = jnp.where(lane >= ahead, line[j], line[j + 1])
                            pieces.append(
                                pltpu.roll(mixed, LANES - (group_rows - 1) + h, axis=1, stride=1, stride_axis=0)
                            )
                        sides.append(jnp.concatenate(pieces, axis=0).astype(jnp.bfloat16))
                    rows.append(jnp.concatenate(sides, axis=1))
            table = jnp.concatenate(rows, axis=0)
            units = jnp.concatenate(
                [
                    jnp.concatenate([wide_ref[pair, :, LANES * v : LANES * (v + 1)] for v in PHASE_COLUMNS[r]], axis=1)
                    for r in range(S)
                ],
                axis=0,
            )
            products = jnp.dot(units, table, preferred_element_type=jnp.float32)
            for r in range(S):
                factor = factor_ref[r, pair : pair + 1, pl.ds(begin, tile)]
                scaled = products[r * count : (r + 1) * count] * factor
                where = (slice(r * count, (r + 1) * count), slice(n * tile, (n + 1) * tile))
                if pair == 0:
                    sum_ref[where] = scaled if extra[r] is None else scaled + extra[r]
                else:
                    sum_ref[where] += scaled
    other = pl.multiple_of((1 - mine) * half, LANES)
    own = pl.multiple_of(mine * half, LANES)
    width = S * half
    row = iota((width, 1), 0)
    pick = jnp.where(iota((width, width), 1) == S * (row % half) + row // half, 1.0, 0.0).astype(jnp.bfloat16)
    halves = [
        jnp.concatenate([sum_ref[r * count : (r + 1) * count, pl.ds(at, half)] for r in range(S)], axis=1) for at in (other, own)
    ]
    pieces = [x.astype(jnp.bfloat16) for x in halves]
    if precise:
        pieces.append((halves[1] - pieces[1].astype(jnp.float32)).astype(jnp.bfloat16))
    moved = jnp.dot(jnp.concatenate(pieces, axis=0), pick, preferred_element_type=jnp.float32)
    away_ref[...] = moved[:count].astype(jnp.bfloat16)
    kept = moved[count : 2 * count]
    keep_ref[...] = kept + moved[2 * count :] if precise else kept.astype(jnp.bfloat16)


def arriving(wide_ref, held_ref, arrived):
    copies = [
        pltpu.make_async_copy(wide_ref.at[at : at + BATCH], held_ref.at[at : at + BATCH], arrived.at[at // BATCH])
        for at in range(0, wide_ref.shape[0], BATCH)
    ]
    for copy in copies:
        copy.start()
    return copies


def first_kernel(blocks, lags, precise, scal_ref, offsets_ref, weights_ref, wide_ref, last_ref, *refs):
    block_refs = refs[: blocks + 1]
    phases_ref, ahead_ref, factor_ref, away_ref, keep_ref, raw_ref, held_ref, sum_ref, arrived = refs[blocks + 1 :]
    copies = arriving(wide_ref, held_ref, arrived)
    records(scal_ref, offsets_ref, weights_ref, block_refs, phases_ref, ahead_ref, factor_ref, raw_ref)
    chunk_sum(
        lags, precise, scal_ref[1], scal_ref[2], copies, held_ref, last_ref, phases_ref, ahead_ref, factor_ref, away_ref, keep_ref, sum_ref
    )


def later_kernel(lags, precise, scal_ref, wide_ref, last_ref, phases_ref, ahead_ref, factor_ref, away_ref, keep_ref, held_ref, sum_ref, arrived):
    copies = arriving(wide_ref, held_ref, arrived)
    chunk_sum(
        lags, precise, scal_ref[1], scal_ref[2], copies, held_ref, last_ref, phases_ref, ahead_ref, factor_ref, away_ref, keep_ref, sum_ref
    )


def sums_of(lags, precise, wide):
    pairs, count, columns = wide.shape
    shapes = (
        jax.ShapeDtypeStruct((count, lags // 2), jnp.bfloat16),
        jax.ShapeDtypeStruct((count, lags // 2), jnp.float32 if precise else jnp.bfloat16),
    )
    scratch = [
        pltpu.VMEM((pairs, count, columns), jnp.bfloat16),
        pltpu.VMEM((S * count, lags // S), jnp.float32),
        pltpu.SemaphoreType.DMA((pairs // BATCH,)),
    ]
    params = dict(
        compiler_params=pltpu.CompilerParams(vmem_limit_bytes=24 << 20),
        cost_estimate=pl.CostEstimate(flops=2 * count * pairs * 256 * lags, bytes_accessed=8 * 10**6, transcendentals=0),
    )
    return shapes, scratch, params


def first_sums(lags, precise, scal, offsets, weights, wide, last, blocks, tail):
    comps, stations, width = blocks[0].shape
    pairs = comps * stations
    parts = (len(blocks) * width + tail.shape[-1]) // (S * LANES)
    full = parts * LANES
    shapes, scratch, params = sums_of(lags, precise, wide)
    return pl.pallas_call(
        functools.partial(first_kernel, len(blocks), lags, precise),
        out_shape=tuple(jax.ShapeDtypeStruct((n, pairs, full), jnp.float32) for n in (S, S - 1, S)) + shapes,
        in_specs=[SMEM, SMEM, SMEM, HBM, VMEM] + [VMEM] * (len(blocks) + 1),
        out_specs=(VMEM,) * 5,
        scratch_shapes=[pltpu.VMEM((parts, pairs, S * LANES), jnp.float32)] + scratch,
        name="records_chunk",
        **params,
    )(scal, offsets, weights, in_hbm(wide), last, *blocks, tail)


def later_sums(lags, precise, scal, wide, last, tables):
    shapes, scratch, params = sums_of(lags, precise, wide)
    return pl.pallas_call(
        functools.partial(later_kernel, lags, precise),
        out_shape=shapes,
        in_specs=[SMEM, HBM] + [VMEM] * 4,
        out_specs=(VMEM, VMEM),
        scratch_shapes=scratch,
        name="chunk",
        **params,
    )(scal, in_hbm(wide), last, *tables)


def shards(templates, data, tail, offsets, weights, mask):
    owners = lax.axis_size("tmpl")
    sides = lax.axis_size("sta")
    span = data.shape[-1]
    lags = owners * span // sides
    place = lax.axis_index("tmpl")
    side = lax.axis_index("sta")
    core = lax.axis_index("comp")
    block = jnp.transpose(data, (1, 0, 2))
    closing = jnp.transpose(tail, (1, 0, 2))
    if owners <= 4:
        blocks = [block] + [
            lax.ppermute(block, "tmpl", [(i, (i - d) % owners) for i in range(owners)]) for d in range(1, owners)
        ]
    else:
        gathered = lax.all_gather(block, "tmpl", axis=0, tiled=False)
        blocks = [lax.dynamic_index_in_dim(gathered, lax.rem(place + d, owners), 0, False) for d in range(owners)]
    wide, last = templates_prepared(templates, mask)
    gotten = []
    both = None
    for d in range(1, sides + 1):
        chunk = lax.rem(side + d, sides)
        if both is not None:
            chunk, _ = lax.optimization_barrier((chunk, both))
        scal = jnp.stack([place, chunk, core]).astype(jnp.int32)
        precise = d == sides
        if d == 1:
            *tables, away, keep = first_sums(lags, precise, scal, offsets, weights, wide, last, blocks, closing)
        else:
            away, keep = later_sums(lags, precise, scal, wide, last, tables)
        got = lax.ppermute(away, "comp", [(0, 1), (1, 0)])
        if d < sides:
            both = (keep.astype(jnp.float32) + got.astype(jnp.float32)).astype(jnp.bfloat16)
            gotten.append(lax.ppermute(both, "sta", [(i, (i + d) % sides) for i in range(sides)]))
    total = keep
    for term in gotten:
        total = total + term.astype(jnp.float32)
    if gotten:
        total = lax.optimization_barrier(total)
    return total + got.astype(jnp.float32)


def solution(mesh):
    in_specs = (
        P(("groups", "tmpl"), ("sta", "comp"), None, None),
        P(("groups", "sta", "comp"), None, "tmpl"),
        P(("groups", "sta", "comp"), None, None),
        P(("groups", "sta", "comp")),
        P(("groups", "sta", "comp")),
        P(("groups", "tmpl"), ("sta", "comp")),
    )
    out_specs = P(("groups", "tmpl"), ("sta", "comp"))
    return jax.shard_map(shards, mesh=mesh, in_specs=in_specs, out_specs=out_specs, check_vma=False)
```

```python
import functools

import jax
import jax.numpy as jnp
from jax import lax
from jax.experimental import pallas as pl
from jax.experimental.pallas import tpu as pltpu
from jax.sharding import PartitionSpec as P

EPS = 1e-05
S = 4
LANES = 128
VMEM = pl.BlockSpec(memory_space=pltpu.VMEM)
HBM = pl.BlockSpec(memory_space=pltpu.HBM)
SMEM = pl.BlockSpec(memory_space=pltpu.SMEM)
PIECES = (((0, 0), (1, 0)), ((2, 0), (3, 0)), ((2, 1), (3, 1)), ((3, 1), (0, 0)), ((1, 0), (2, 0)), ((1, 1), (2, 1)))
PHASE_COLUMNS = ((0, 1), (3, 4), (2, 0), (5, 3))


def iota(shape, axis):
    return lax.broadcasted_iota(jnp.int32, shape, axis)


def template_kernel(source_ref, mask_ref, wide_ref, last_ref, x_ref, unit_ref, rows_ref, flag_ref, arrived):
    count, comps, stations, length = x_ref.shape
    pairs = comps * stations
    group = 8
    quarter = count // 4
    copies = [
        pltpu.make_async_copy(
            source_ref.at[i * quarter : (i + 1) * quarter], x_ref.at[i * quarter : (i + 1) * quarter], arrived.at[i]
        )
        for i in range(4)
    ]
    flags = pltpu.make_async_copy(mask_ref, flag_ref, arrived.at[4])
    for copy in copies + [flags]:
        copy.start()
    for at in range(0, count, group):
        if at % quarter == 0:
            copies[at // quarter].wait()
        values = x_ref[at : at + group].astype(jnp.float32).reshape(group * pairs, length)
        centred = values - jnp.sum(values, axis=-1, keepdims=True) * (1.0 / length)
        spread = jnp.sum(centred * centred, axis=-1, keepdims=True) * (1.0 / length)
        unit = centred * lax.rsqrt(spread + EPS)
        for h in range(length // LANES):
            unit_ref[h, at * pairs : (at + group) * pairs, :] = unit[:, LANES * h : LANES * (h + 1)]
    flags.wait()
    available = jnp.transpose(flag_ref[...].astype(jnp.float32))
    for s in range(stations):
        column = available[:, s : s + 1]
        for c in range(comps):
            pair = c * stations + s
            rows = jnp.concatenate(
                [unit_ref[h, pl.ds(pair, count, stride=pairs), :] for h in range(length // LANES)], axis=1
            )
            rows_ref[pair * count : (pair + 1) * count, :] = (rows * column).astype(jnp.bfloat16)
    group_rows = length // S
    sample = iota((length, LANES), 0)
    lane = iota((length, LANES), 1)
    place = lane % group_rows
    first = lane < group_rows
    lane_row = iota((count, LANES), 1)
    last = jnp.zeros((count, LANES), jnp.float32)
    wanted = []
    for low, high in PIECES:
        base = jnp.where(first, low[0] - S * low[1], high[0] - S * high[1])
        wanted.append(jnp.where(sample == S * (group_rows - 1 - place) + base, 1.0, 0.0).astype(jnp.bfloat16))
    batch = 8
    for at in range(0, pairs, batch):
        span = rows_ref[at * count : (at + batch) * count, :]
        for v in range(0, len(PIECES), 2):
            moved = jnp.dot(span, jnp.concatenate(wanted[v : v + 2], axis=1), preferred_element_type=jnp.float32)
            for i in range(batch):
                part = moved[i * count : (i + 1) * count]
                wide_ref[at + i, :, LANES * v : LANES * v + 2 * LANES] = part.astype(jnp.bfloat16)
                pair = at + i
                if v == 0:
                    turned = pltpu.roll(part[:, LANES:], (pair - 32) % LANES, axis=1)
                    last = jnp.where(lane_row == 32 + pair, turned, last)
                if v == 4:
                    turned = pltpu.roll(part[:, :LANES], pair, axis=1)
                    last = jnp.where((lane_row == pair) | (lane_row == 64 + pair), turned, last)
    last_ref[...] = last.astype(jnp.bfloat16)


def in_hbm(x):
    return pltpu.with_memory_space_constraint(x, pltpu.HBM)


def templates_prepared(templates, mask):
    count, stations, comps, length = templates.shape
    pairs = stations * comps
    wide = (pairs, count, LANES * len(PIECES))
    wide, last = pl.pallas_call(
        template_kernel,
        out_shape=(jax.ShapeDtypeStruct(wide, jnp.bfloat16), jax.ShapeDtypeStruct((count, LANES), jnp.bfloat16)),
        in_specs=[HBM, HBM],
        out_specs=(VMEM, VMEM),
        scratch_shapes=[
            pltpu.VMEM((count, comps, stations, length), jnp.bfloat16),
            pltpu.VMEM((length // LANES, pairs * count, LANES), jnp.float32),
            pltpu.VMEM((pairs * count, length), jnp.bfloat16),
            pltpu.VMEM((stations, count), jnp.int32),
            pltpu.SemaphoreType.DMA((5,)),
        ],
        compiler_params=pltpu.CompilerParams(vmem_limit_bytes=16 << 20),
        cost_estimate=pl.CostEstimate(flops=2 * 10**9, bytes_accessed=8 * 10**6, transcendentals=0),
        name="templates",
    )(in_hbm(jnp.transpose(templates, (0, 2, 1, 3))), in_hbm(jnp.transpose(mask)))
    return wide, last


def later(x, by):
    return pltpu.roll(x, x.shape[-1] - by, axis=1)


def records(scal_ref, offsets_ref, weights_ref, block_refs, phases_ref, ahead_ref, factor_ref, raw_ref):
    blocks = len(block_refs) - 1
    comps, stations, width = block_refs[0].shape
    pairs = comps * stations
    unitw = S * LANES
    per = width // unitw
    for i in range(blocks + 1):
        values = block_refs[i][...].astype(jnp.float32).reshape(pairs, block_refs[i].shape[-1])
        home = blocks if i == blocks else lax.rem(scal_ref[0] + i, blocks)
        for j in range(block_refs[i].shape[-1] // unitw):
            raw_ref[home * per + j] = values[:, unitw * j : unitw * (j + 1)]
    parts = raw_ref.shape[0]
    column = iota((1, unitw), 1)
    pick = jnp.where(iota((unitw, unitw), 0) == S * (column % LANES) + column // LANES, 1.0, 0.0).astype(jnp.bfloat16)
    flat = raw_ref[...].reshape(parts * pairs, unitw).astype(jnp.bfloat16)
    split = jnp.dot(flat, pick, preferred_element_type=jnp.float32)
    full = parts * LANES
    row = iota((stations, full), 0)
    offset = jnp.zeros((stations, full), jnp.int32)
    weight = jnp.zeros((stations, full), jnp.float32)
    for s in range(stations):
        offset = jnp.where(row == s, offsets_ref[s], offset)
        weight = jnp.where(row == s, weights_ref[s].astype(jnp.float32), weight)
    length = 256
    group_rows = length // S
    for c in range(comps):
        at = c * stations
        v = [
            jnp.concatenate(
                [split[b * pairs + at : b * pairs + at + stations, LANES * p : LANES * (p + 1)] for b in range(parts)], axis=1
            )
            for p in range(S)
        ]
        step = 1
        while S * step < length:
            taken = (offset & (S * step)) != 0
            v = [jnp.where(taken, later(x, step), x) for x in v]
            step *= 2
        for bit in (2, 1):
            taken = (offset & bit) != 0
            v = [jnp.where(taken, v[p + bit] if p + bit < S else later(v[p + bit - S], 1), v[p]) for p in range(S)]
        ahead = [later(x, group_rows) for x in v]
        mean = v[0] + v[1] + v[2] + v[3]
        power = v[0] * v[0] + v[1] * v[1] + v[2] * v[2] + v[3] * v[3]
        step = 1
        while step < group_rows:
            mean = mean + later(mean, step)
            power = power + later(power, step)
            step *= 2
        for r in range(S):
            middle = mean * (1.0 / length)
            spread = power * (1.0 / length) - middle * middle
            factor_ref[r, at : at + stations, :] = weight / (length * jnp.sqrt(spread + EPS))
            if r + 1 < S:
                mean = mean + (ahead[r] - v[r])
                power = power + (ahead[r] * ahead[r] - v[r] * v[r])
                ahead_ref[r, at : at + stations, :] = ahead[r]
            phases_ref[r, at : at + stations, :] = v[r]


def chunk_sum(lags, precise, chunk, mine, wide_ref, last_ref, phases_ref, ahead_ref, factor_ref, away_ref, keep_ref, sum_ref):
    pairs, count, _ = wide_ref.shape
    group_rows = 64
    half = lags // S // 2
    start = pl.multiple_of(chunk * (lags // S), LANES)
    lane = iota((8, LANES), 1)
    sub = iota((8, LANES), 0)
    tile = 2 * LANES
    for n in range(lags // S // tile):
        begin = start + n * tile
        begin = pl.multiple_of(begin, LANES)

        def factor_of(r, row):
            return factor_ref[r, row, pl.ds(begin, tile)]

        extra = []
        for r in range(S):
            held = {}
            for i in range(3):
                j = i - (3 - r)
                if j >= 0:
                    scaled = ahead_ref[j, :, pl.ds(begin, tile)] * factor_ref[r, :, pl.ds(begin, tile)]
                    held[i] = jnp.concatenate([scaled, jnp.zeros((32 - pairs, tile), jnp.float32)], axis=0)
            if held:
                none = jnp.zeros((32, tile), jnp.float32)
                table = jnp.concatenate([held.get(0, none), held.get(2, none), held.get(1, none), none], axis=0)
                extra.append(jnp.dot(last_ref[...], table.astype(jnp.bfloat16), preferred_element_type=jnp.float32))
            else:
                extra.append(None)
        for pair in range(pairs):
            rows = []
            for p in range(S):
                line = [
                    jnp.broadcast_to(phases_ref[p, pair : pair + 1, pl.ds(begin + LANES * j, LANES)], (8, LANES))
                    for j in range(3)
                ]
                for g in range(0, group_rows, 16):
                    sides = []
                    for j in range(2):
                        pieces = []
                        for h in (g, g + 8):
                            ahead = group_rows - 1 - h - sub
                            mixed = jnp.where(lane >= ahead, line[j], line[j + 1])
                            pieces.append(
                                pltpu.roll(mixed, LANES - (group_rows - 1) + h, axis=1, stride=1, stride_axis=0)
                            )
                        sides.append(jnp.concatenate(pieces, axis=0).astype(jnp.bfloat16))
                    rows.append(jnp.concatenate(sides, axis=1))
            table = jnp.concatenate(rows, axis=0)
            units = jnp.concatenate(
                [
                    jnp.concatenate([wide_ref[pair, :, LANES * v : LANES * (v + 1)] for v in PHASE_COLUMNS[r]], axis=1)
                    for r in range(S)
                ],
                axis=0,
            )
            products = jnp.dot(units, table, preferred_element_type=jnp.float32)
            for r in range(S):
                factor = factor_ref[r, pair : pair + 1, pl.ds(begin, tile)]
                scaled = products[r * count : (r + 1) * count] * factor
                where = (slice(r * count, (r + 1) * count), slice(n * tile, (n + 1) * tile))
                if pair == 0:
                    sum_ref[where] = scaled if extra[r] is None else scaled + extra[r]
                else:
                    sum_ref[where] += scaled
    other = pl.multiple_of((1 - mine) * half, LANES)
    own = pl.multiple_of(mine * half, LANES)
    width = S * half
    row = iota((width, 1), 0)
    pick = jnp.where(iota((width, width), 1) == S * (row % half) + row // half, 1.0, 0.0).astype(jnp.bfloat16)
    halves = [
        jnp.concatenate([sum_ref[r * count : (r + 1) * count, pl.ds(at, half)] for r in range(S)], axis=1) for at in (other, own)
    ]
    pieces = [x.astype(jnp.bfloat16) for x in halves]
    if precise:
        pieces.append((halves[1] - pieces[1].astype(jnp.float32)).astype(jnp.bfloat16))
    moved = jnp.dot(jnp.concatenate(pieces, axis=0), pick, preferred_element_type=jnp.float32)
    away_ref[...] = moved[:count].astype(jnp.bfloat16)
    kept = moved[count : 2 * count]
    keep_ref[...] = kept + moved[2 * count :] if precise else kept.astype(jnp.bfloat16)


def first_kernel(blocks, lags, precise, step, sides, scal_ref, offsets_ref, weights_ref, wide_ref, last_ref, *refs):
    block_refs = refs[: blocks + 1]
    phases_ref, ahead_ref, factor_ref, away_ref, keep_ref, raw_ref, sum_ref = refs[blocks + 1 :]
    records(scal_ref, offsets_ref, weights_ref, block_refs, phases_ref, ahead_ref, factor_ref, raw_ref)
    chunk_sum(
        lags, precise, lax.rem(scal_ref[1] + step, sides), scal_ref[2], wide_ref, last_ref, phases_ref, ahead_ref, factor_ref, away_ref, keep_ref, sum_ref
    )


def later_kernel(lags, precise, step, sides, scal_ref, wide_ref, last_ref, phases_ref, ahead_ref, factor_ref, away_ref, keep_ref, sum_ref):
    chunk_sum(
        lags, precise, lax.rem(scal_ref[1] + step, sides), scal_ref[2], wide_ref, last_ref, phases_ref, ahead_ref, factor_ref, away_ref, keep_ref, sum_ref
    )


def sums_of(lags, precise, wide):
    pairs, count, columns = wide.shape
    shapes = (
        jax.ShapeDtypeStruct((count, lags // 2), jnp.bfloat16),
        jax.ShapeDtypeStruct((count, lags // 2), jnp.float32 if precise else jnp.bfloat16),
    )
    scratch = [
        pltpu.VMEM((S * count, lags // S), jnp.float32),
    ]
    params = dict(
        compiler_params=pltpu.CompilerParams(vmem_limit_bytes=16 << 20),
        cost_estimate=pl.CostEstimate(flops=2 * count * pairs * 256 * lags, bytes_accessed=8 * 10**6, transcendentals=0),
    )
    return shapes, scratch, params


def first_sums(lags, precise, step, sides, scal, offsets, weights, wide, last, blocks, tail):
    comps, stations, width = blocks[0].shape
    pairs = comps * stations
    parts = (len(blocks) * width + tail.shape[-1]) // (S * LANES)
    full = parts * LANES
    shapes, scratch, params = sums_of(lags, precise, wide)
    return pl.pallas_call(
        functools.partial(first_kernel, len(blocks), lags, precise, step, sides),
        out_shape=tuple(jax.ShapeDtypeStruct((n, pairs, full), jnp.float32) for n in (S, S - 1, S)) + shapes,
        in_specs=[SMEM, SMEM, SMEM, VMEM, VMEM] + [VMEM] * (len(blocks) + 1),
        out_specs=(VMEM,) * 5,
        scratch_shapes=[pltpu.VMEM((parts, pairs, S * LANES), jnp.float32)] + scratch,
        name="records_chunk",
        **params,
    )(scal, offsets, weights, wide, last, *blocks, tail)


def later_sums(lags, precise, step, sides, scal, wide, last, tables):
    shapes, scratch, params = sums_of(lags, precise, wide)
    return pl.pallas_call(
        functools.partial(later_kernel, lags, precise, step, sides),
        out_shape=shapes,
        in_specs=[SMEM, VMEM] + [VMEM] * 4,
        out_specs=(VMEM, VMEM),
        scratch_shapes=scratch,
        name="chunk",
        **params,
    )(scal, wide, last, *tables)


def shards(templates, data, tail, offsets, weights, mask):
    owners = lax.axis_size("tmpl")
    sides = lax.axis_size("sta")
    span = data.shape[-1]
    lags = owners * span // sides
    place = lax.axis_index("tmpl")
    side = lax.axis_index("sta")
    core = lax.axis_index("comp")
    block = jnp.transpose(data, (1, 0, 2))
    closing = jnp.transpose(tail, (1, 0, 2))
    if owners <= 4:
        blocks = [block] + [
            lax.ppermute(block, "tmpl", [(i, (i - d) % owners) for i in range(owners)]) for d in range(1, owners)
        ]
    else:
        gathered = lax.all_gather(block, "tmpl", axis=0, tiled=False)
        blocks = [lax.dynamic_index_in_dim(gathered, lax.rem(place + d, owners), 0, False) for d in range(owners)]
    wide, last = templates_prepared(templates, mask)
    gotten = []
    scal = jnp.stack([place, side, core]).astype(jnp.int32)
    for d in range(1, sides + 1):
        precise = d == sides
        if d == 1:
            *tables, away, keep = first_sums(lags, precise, d, sides, scal, offsets, weights, wide, last, blocks, closing)
        else:
            scal, _ = lax.optimization_barrier((scal, both))
            away, keep = later_sums(lags, precise, d, sides, scal, wide, last, tables)
        got = lax.ppermute(away, "comp", [(0, 1), (1, 0)])
        if d < sides:
            both = (keep.astype(jnp.float32) + got.astype(jnp.float32)).astype(jnp.bfloat16)
            gotten.append(lax.ppermute(both, "sta", [(i, (i + d) % sides) for i in range(sides)]))
    total = keep
    for term in gotten:
        total = total + term.astype(jnp.float32)
    if gotten:
        total = lax.optimization_barrier(total)
    return total + got.astype(jnp.float32)


def solution(mesh):
    in_specs = (
        P(("groups", "tmpl"), ("sta", "comp"), None, None),
        P(("groups", "sta", "comp"), None, "tmpl"),
        P(("groups", "sta", "comp"), None, None),
        P(("groups", "sta", "comp")),
        P(("groups", "sta", "comp")),
        P(("groups", "tmpl"), ("sta", "comp")),
    )
    out_specs = P(("groups", "tmpl"), ("sta", "comp"))
    return jax.shard_map(shards, mesh=mesh, in_specs=in_specs, out_specs=out_specs, check_vma=False)
```

```python
import functools

import jax
import jax.numpy as jnp
from jax import lax
from jax.experimental import pallas as pl
from jax.experimental.pallas import tpu as pltpu
from jax.sharding import PartitionSpec as P

EPS = 1e-05
S = 2
LANES = 128
LENGTH = S * LANES
TILE = 2 * LANES
VMEM = pl.BlockSpec(memory_space=pltpu.VMEM)
SMEM = pl.BlockSpec(memory_space=pltpu.SMEM)
PHASE_PIECES = ((0, 1), (2, 0))


def iota(shape, axis):
    return lax.broadcasted_iota(jnp.int32, shape, axis)


def ones_where(condition):
    return jnp.where(condition, 1.0, 0.0).astype(jnp.bfloat16)


def later(x, by):
    return pltpu.roll(x, x.shape[-1] - by, axis=1)


def template_kernel(x_ref, mask_ref, order_ref, wide_ref, last_ref, unit_ref, rows_ref):
    count, comps, stations, length = x_ref.shape
    pairs = comps * stations
    group = min(8, count)
    lane = iota((count, LANES), 1)
    last = jnp.zeros((count, LANES), jnp.float32)
    available = jnp.transpose(mask_ref[...].astype(jnp.float32))
    for at in range(0, count, group):
        values = x_ref[at : at + group].astype(jnp.float32).reshape(group * pairs, length)
        centred = values - jnp.sum(values, axis=-1, keepdims=True) * (1.0 / length)
        spread = jnp.sum(centred * centred, axis=-1, keepdims=True) * (1.0 / length)
        unit = centred * lax.rsqrt(spread + EPS)
        for h in range(length // LANES):
            unit_ref[h, at * pairs : (at + group) * pairs, :] = unit[:, LANES * h : LANES * (h + 1)]
    for s in range(stations):
        column = available[:, s : s + 1]
        for c in range(comps):
            pair = c * stations + s
            rows = jnp.concatenate(
                [unit_ref[h, pl.ds(pair, count, stride=pairs), :] for h in range(length // LANES)], axis=1
            )
            rows_ref[pair * count : (pair + 1) * count, :] = (rows * column).astype(jnp.bfloat16)
    batch = 8
    for at in range(0, pairs, batch):
        moved = jnp.dot(rows_ref[at * count : (at + batch) * count, :], order_ref[...], preferred_element_type=jnp.float32)
        for i in range(batch):
            pair = at + i
            even = moved[i * count : (i + 1) * count, :LANES]
            odd = moved[i * count : (i + 1) * count, LANES:]
            wide_ref[pair, 0] = even.astype(jnp.bfloat16)
            wide_ref[pair, 1] = odd.astype(jnp.bfloat16)
            wide_ref[pair, 2] = jnp.where(lane == LANES - 1, 0.0, later(odd, 1)).astype(jnp.bfloat16)
            last = jnp.where(lane == pair, pltpu.roll(odd, pair, axis=1), last)
    last_ref[...] = last.astype(jnp.bfloat16)


def templates_prepared(templates, mask, order):
    count, stations, comps, length = templates.shape
    pairs = stations * comps
    return pl.pallas_call(
        template_kernel,
        out_shape=(
            jax.ShapeDtypeStruct((pairs, 3, count, LANES), jnp.bfloat16),
            jax.ShapeDtypeStruct((count, LANES), jnp.bfloat16),
        ),
        in_specs=[VMEM, VMEM, VMEM],
        out_specs=(VMEM, VMEM),
        scratch_shapes=[
            pltpu.VMEM((length // LANES, pairs * count, LANES), jnp.float32),
            pltpu.VMEM((pairs * count, length), jnp.bfloat16),
        ],
        compiler_params=pltpu.CompilerParams(vmem_limit_bytes=16 << 20),
        cost_estimate=pl.CostEstimate(flops=2 * 10**9, bytes_accessed=8 * 10**6, transcendentals=0),
        name="templates",
    )(jnp.transpose(templates, (0, 2, 1, 3)), jnp.transpose(mask), order)


def records(offsets_ref, weights_ref, split_ref, block_refs, phases_ref, factor_ref, raw_ref):
    blocks = len(block_refs) - 1
    comps, stations, width = block_refs[0].shape
    pairs = comps * stations
    unit = S * LANES
    per = width // unit
    for i in range(blocks + 1):
        values = block_refs[i][...].astype(jnp.float32).reshape(pairs, block_refs[i].shape[-1])
        home = blocks if i == blocks else lax.rem(lax.axis_index("tmpl") + i, blocks)
        for j in range(block_refs[i].shape[-1] // unit):
            raw_ref[home * per + j] = values[:, unit * j : unit * (j + 1)]
    parts = raw_ref.shape[0]
    flat = raw_ref[...].reshape(parts * pairs, unit).astype(jnp.bfloat16)
    split = jnp.dot(flat, split_ref[...], preferred_element_type=jnp.float32)
    full = parts * LANES
    row = iota((stations, full), 0)
    offset = jnp.zeros((stations, full), jnp.int32)
    weight = jnp.zeros((stations, full), jnp.float32)
    for s in range(stations):
        offset = jnp.where(row == s, offsets_ref[s], offset)
        weight = jnp.where(row == s, weights_ref[s].astype(jnp.float32), weight)
    for c in range(comps):
        at = c * stations
        v = [
            jnp.concatenate(
                [split[b * pairs + at : b * pairs + at + stations, LANES * p : LANES * (p + 1)] for b in range(parts)], axis=1
            )
            for p in range(S)
        ]
        step = 1
        while S * step < LENGTH:
            taken = (offset & (S * step)) != 0
            v = [jnp.where(taken, later(x, step), x) for x in v]
            step *= 2
        taken = (offset & 1) != 0
        v = [jnp.where(taken, v[1], v[0]), jnp.where(taken, later(v[0], 1), v[1])]
        mean = v[0] + v[1]
        power = v[0] * v[0] + v[1] * v[1]
        step = 1
        while step < LANES:
            mean = mean + later(mean, step)
            power = power + later(power, step)
            step *= 2
        ahead = later(v[0], LANES)
        for r in range(S):
            middle = mean * (1.0 / LENGTH)
            spread = power * (1.0 / LENGTH) - middle * middle
            factor_ref[r, at : at + stations, :] = weight / (LENGTH * jnp.sqrt(spread + EPS))
            phases_ref[r, at : at + stations, :] = v[r]
            mean = mean + (ahead - v[0])
            power = power + (ahead * ahead - v[0] * v[0])


def owner_sum(lags, precise, step, sides, away, restore_ref, wide_ref, last_ref, phases_ref, factor_ref, out_ref, sum_ref):
    pairs, _, count, _ = wide_ref.shape
    side, core = lax.rem(lax.axis_index("sta") + step, sides), lax.axis_index("comp")
    owner = 2 * side + (1 - core if away else core)
    lane = iota((8, LANES), 1)
    sub = iota((8, LANES), 0)
    width = lags // S
    for n in range(width // TILE):
        begin = pl.multiple_of(owner * width + n * TILE, LANES)
        extra = phases_ref[0, :, pl.ds(begin + LANES, TILE)] * factor_ref[1, :, pl.ds(begin, TILE)]
        extra = jnp.concatenate([extra, jnp.zeros((LANES - pairs, TILE), jnp.float32)], axis=0).astype(jnp.bfloat16)
        past = jnp.dot(last_ref[...], extra, preferred_element_type=jnp.float32)
        for pair in range(pairs):
            rows = []
            for p in range(S):
                line = [
                    jnp.broadcast_to(phases_ref[p, pair : pair + 1, pl.ds(begin + LANES * j, LANES)], (8, LANES))
                    for j in range(3)
                ]
                for g in range(0, LANES, 16):
                    sides_of = []
                    for j in range(2):
                        pieces = []
                        for h in (g, g + 8):
                            mixed = jnp.where(lane >= LANES - 1 - h - sub, line[j], line[j + 1])
                            pieces.append(pltpu.roll(mixed, 1 + h, axis=1, stride=1, stride_axis=0))
                        sides_of.append(jnp.concatenate(pieces, axis=0).astype(jnp.bfloat16))
                    rows.append(jnp.concatenate(sides_of, axis=1))
            table = jnp.concatenate(rows, axis=0)
            units = jnp.concatenate(
                [jnp.concatenate([wide_ref[pair, v] for v in PHASE_PIECES[r]], axis=1) for r in range(S)], axis=0
            )
            products = jnp.dot(units, table, preferred_element_type=jnp.float32)
            for r in range(S):
                scaled = products[r * count : (r + 1) * count] * factor_ref[r, pair : pair + 1, pl.ds(begin, TILE)]
                where = (slice(r * count, (r + 1) * count), slice(n * TILE, (n + 1) * TILE))
                if pair:
                    sum_ref[where] += scaled
                else:
                    sum_ref[where] = scaled + past if r == 1 else scaled
    total = jnp.concatenate([sum_ref[r * count : (r + 1) * count, :] for r in range(S)], axis=1)
    pieces = [total.astype(jnp.bfloat16)]
    if precise:
        pieces.append((total - pieces[0].astype(jnp.float32)).astype(jnp.bfloat16))
    moved = jnp.dot(jnp.concatenate(pieces, axis=0), restore_ref[...], preferred_element_type=jnp.float32)
    out_ref[...] = moved[:count] + moved[count:] if precise else moved.astype(jnp.bfloat16)


def first_kernel(blocks, static, offsets_ref, weights_ref, split_ref, restore_ref, wide_ref, last_ref, *refs):
    block_refs = refs[: blocks + 1]
    phases_ref, factor_ref, out_ref, raw_ref, sum_ref = refs[blocks + 1 :]
    records(offsets_ref, weights_ref, split_ref, block_refs, phases_ref, factor_ref, raw_ref)
    owner_sum(*static, restore_ref, wide_ref, last_ref, phases_ref, factor_ref, out_ref, sum_ref)


def later_kernel(static, *refs):
    owner_sum(*static, *refs)


def call_parts(static, wide):
    lags, precise = static[:2]
    pairs, _, count, _ = wide.shape
    shape = jax.ShapeDtypeStruct((count, lags), jnp.float32 if precise else jnp.bfloat16)
    scratch = pltpu.VMEM((S * count, lags // S), jnp.float32)
    params = dict(
        compiler_params=pltpu.CompilerParams(vmem_limit_bytes=16 << 20),
        cost_estimate=pl.CostEstimate(flops=2 * count * pairs * LENGTH * lags, bytes_accessed=4 * 10**6, transcendentals=0),
    )
    return shape, scratch, params


def first_sum(static, offsets, weights, split, restore, wide, last, blocks, tail):
    comps, stations, width = blocks[0].shape
    pairs = comps * stations
    parts = (len(blocks) * width + tail.shape[-1]) // (S * LANES)
    table = jax.ShapeDtypeStruct((S, pairs, parts * LANES), jnp.float32)
    shape, scratch, params = call_parts(static, wide)
    return pl.pallas_call(
        functools.partial(first_kernel, len(blocks), static),
        out_shape=(table, table, shape),
        in_specs=[SMEM, SMEM] + [VMEM] * 4 + [VMEM] * (len(blocks) + 1),
        out_specs=(VMEM,) * 3,
        scratch_shapes=[pltpu.VMEM((parts, pairs, S * LANES), jnp.float32), scratch],
        name="records_sum",
        **params,
    )(offsets, weights, split, restore, wide, last, *blocks, tail)


def later_sum(static, restore, wide, last, tables):
    shape, scratch, params = call_parts(static, wide)
    return pl.pallas_call(
        functools.partial(later_kernel, static),
        out_shape=shape,
        in_specs=[VMEM] * 5,
        out_specs=VMEM,
        scratch_shapes=[scratch],
        name="sum",
        **params,
    )(restore, wide, last, *tables)


def pick_kernel(restore_ref, split_ref, order_ref):
    lags = restore_ref.shape[0]
    width = lags // S
    row = iota((lags, 1), 0)
    restore_ref[...] = ones_where(iota((lags, lags), 1) == S * (row % width) + row // width)
    sample = iota((LENGTH, LENGTH), 0)
    column = iota((1, LENGTH), 1)
    split_ref[...] = ones_where(sample == S * (column % LANES) + column // LANES)
    order_ref[...] = ones_where(sample == S * (LANES - 1 - column % LANES) + column // LANES)


def picks(lags):
    return pl.pallas_call(
        pick_kernel,
        out_shape=tuple(jax.ShapeDtypeStruct((n, n), jnp.bfloat16) for n in (lags, LENGTH, LENGTH)),
        out_specs=(VMEM,) * 3,
        compiler_params=pltpu.CompilerParams(vmem_limit_bytes=4 << 20),
        cost_estimate=pl.CostEstimate(flops=4 * 10**9, bytes_accessed=4096, transcendentals=0),
        name="picks",
    )()


def shards(templates, data, tail, offsets, weights, mask):
    owners = lax.axis_size("tmpl")
    sides = lax.axis_size("sta")
    lags = owners * data.shape[-1] // (2 * sides)
    block = jnp.transpose(data, (1, 0, 2))
    closing = jnp.transpose(tail, (1, 0, 2))
    restore, split, order = picks(lags)
    if owners <= 4:
        blocks = [block] + [
            lax.ppermute(block, "tmpl", [(i, (i - d) % owners) for i in range(owners)]) for d in range(1, owners)
        ]
    else:
        gathered = lax.all_gather(block, "tmpl", axis=0, tiled=False)
        place = lax.axis_index("tmpl")
        blocks = [lax.dynamic_index_in_dim(gathered, lax.rem(place + d, owners), 0, False) for d in range(owners)]
    wide, last = templates_prepared(templates, mask, order)
    gotten = []
    for d in range(1, sides + 1):
        precise = d == sides
        if d == 1:
            *tables, away = first_sum((lags, False, d, sides, True), offsets, weights, split, restore, wide, last, blocks, closing)
        else:
            held, _ = lax.optimization_barrier((last, both))
            away = later_sum((lags, False, d, sides, True), restore, wide, held, tables)
        got = lax.ppermute(away, "comp", [(0, 1), (1, 0)])
        held, _ = lax.optimization_barrier((last, away))
        keep = later_sum((lags, precise, d, sides, False), restore, wide, held, tables)
        if d < sides:
            both = (keep.astype(jnp.float32) + got.astype(jnp.float32)).astype(jnp.bfloat16)
            gotten.append(lax.ppermute(both, "sta", [(i, (i + d) % sides) for i in range(sides)]))
    total = keep
    for term in gotten:
        total = total + term.astype(jnp.float32)
    if gotten:
        total = lax.optimization_barrier(total)
    return total + got.astype(jnp.float32)


def solution(mesh):
    in_specs = (
        P(("groups", "tmpl"), ("sta", "comp"), None, None),
        P(("groups", "sta", "comp"), None, "tmpl"),
        P(("groups", "sta", "comp"), None, None),
        P(("groups", "sta", "comp")),
        P(("groups", "sta", "comp")),
        P(("groups", "tmpl"), ("sta", "comp")),
    )
    out_specs = P(("groups", "tmpl"), ("sta", "comp"))
    return jax.shard_map(shards, mesh=mesh, in_specs=in_specs, out_specs=out_specs, check_vma=False)
```

```python
import functools

import jax
import jax.numpy as jnp
from jax import lax
from jax.experimental import pallas as pl
from jax.experimental.pallas import tpu as pltpu
from jax.sharding import PartitionSpec as P

EPS = 1e-05
SLOTS = 4
S = 2
LANES = 128
LENGTH = S * LANES
TILE = 2 * LANES
VMEM = pl.BlockSpec(memory_space=pltpu.VMEM)
SMEM = pl.BlockSpec(memory_space=pltpu.SMEM)
PHASE_PIECES = ((0, 1), (2, 0))


def iota(shape, axis):
    return lax.broadcasted_iota(jnp.int32, shape, axis)


def ones_where(condition):
    return jnp.where(condition, 1.0, 0.0).astype(jnp.bfloat16)


def later(x, by):
    return pltpu.roll(x, x.shape[-1] - by, axis=1)


def template_kernel(x_ref, mask_ref, order_ref, wide_ref, last_ref, unit_ref, rows_ref):
    count, comps, stations, length = x_ref.shape
    pairs = comps * stations
    group = min(8, count)
    lane = iota((count, LANES), 1)
    last = jnp.zeros((count, LANES), jnp.float32)
    available = jnp.transpose(mask_ref[...].astype(jnp.float32))
    for at in range(0, count, group):
        values = x_ref[at : at + group].astype(jnp.float32).reshape(group * pairs, length)
        centred = values - jnp.sum(values, axis=-1, keepdims=True) * (1.0 / length)
        spread = jnp.sum(centred * centred, axis=-1, keepdims=True) * (1.0 / length)
        unit = centred * lax.rsqrt(spread + EPS)
        for h in range(length // LANES):
            unit_ref[h, at * pairs : (at + group) * pairs, :] = unit[:, LANES * h : LANES * (h + 1)]
    for s in range(stations):
        column = available[:, s : s + 1]
        for c in range(comps):
            pair = c * stations + s
            rows = jnp.concatenate(
                [unit_ref[h, pl.ds(pair, count, stride=pairs), :] for h in range(length // LANES)], axis=1
            )
            rows_ref[pair * count : (pair + 1) * count, :] = (rows * column).astype(jnp.bfloat16)
    batch = 8
    for at in range(0, pairs, batch):
        moved = jnp.dot(rows_ref[at * count : (at + batch) * count, :], order_ref[...], preferred_element_type=jnp.float32)
        for i in range(batch):
            pair = at + i
            even = moved[i * count : (i + 1) * count, :LANES]
            odd = moved[i * count : (i + 1) * count, LANES:]
            wide_ref[pair, 0] = even.astype(jnp.bfloat16)
            wide_ref[pair, 1] = odd.astype(jnp.bfloat16)
            wide_ref[pair, 2] = jnp.where(lane == LANES - 1, 0.0, later(odd, 1)).astype(jnp.bfloat16)
            slot = SLOTS * (pair % stations) + pair // stations
            last = jnp.where(lane == slot, pltpu.roll(odd, slot, axis=1), last)
    last_ref[...] = last.astype(jnp.bfloat16)


def templates_prepared(templates, mask, order):
    count, stations, comps, length = templates.shape
    pairs = stations * comps
    return pl.pallas_call(
        template_kernel,
        out_shape=(
            jax.ShapeDtypeStruct((pairs, 3, count, LANES), jnp.bfloat16),
            jax.ShapeDtypeStruct((count, LANES), jnp.bfloat16),
        ),
        in_specs=[VMEM, VMEM, VMEM],
        out_specs=(VMEM, VMEM),
        scratch_shapes=[
            pltpu.VMEM((length // LANES, pairs * count, LANES), jnp.float32),
            pltpu.VMEM((pairs * count, length), jnp.bfloat16),
        ],
        compiler_params=pltpu.CompilerParams(vmem_limit_bytes=16 << 20),
        cost_estimate=pl.CostEstimate(flops=2 * 10**9, bytes_accessed=8 * 10**6, transcendentals=0),
        name="templates",
    )(jnp.transpose(templates, (0, 2, 1, 3)), jnp.transpose(mask), order)


def records(offsets_ref, weights_ref, split_ref, band_ref, block_refs, phases_ref, factor_ref, raw_ref):
    blocks = len(block_refs) - 1
    comps, stations, width = block_refs[0].shape
    rows = stations * SLOTS
    per = width // LENGTH
    for i in range(blocks + 1):
        home = blocks if i == blocks else lax.rem(lax.axis_index("tmpl") + i, blocks)
        for j in range(block_refs[i].shape[-1] // LANES):
            for c in range(SLOTS):
                if c < comps:
                    values = block_refs[i][c, :, LANES * j : LANES * (j + 1)].astype(jnp.float32)
                else:
                    values = jnp.zeros((stations, LANES), jnp.float32)
                raw_ref[home * per * S + j, pl.ds(c, stations, stride=SLOTS), :] = values
    parts = raw_ref.shape[0] // S
    flat = jnp.concatenate(
        [jnp.concatenate([raw_ref[S * b + i] for i in range(S)], axis=1) for b in range(parts)], axis=0
    ).astype(jnp.bfloat16)
    split = jnp.dot(flat, split_ref[...], preferred_element_type=jnp.float32)
    lane = iota((8, LANES), 1)
    first = iota((8, LANES), 0) < SLOTS
    groups = rows // 8
    v = [[], []]
    for q in range(groups):
        offset = [offsets_ref[2 * q], offsets_ref[2 * q + 1]]
        odd = jnp.where(first, offset[0] & 1, offset[1] & 1) != 0
        held = [[split[b * rows + 8 * q : b * rows + 8 * q + 8, LANES * p : LANES * (p + 1)] for b in range(parts)] for p in range(S)]
        for p in range(S):
            source = [jnp.where(odd, held[1 - p][b], held[p][b]) for b in range(parts)]
            by = [(o + p) // S for o in offset]
            turned = [
                jnp.where(first, pltpu.roll(x, (LANES - by[0]) % LANES, axis=1), pltpu.roll(x, (LANES - by[1]) % LANES, axis=1))
                for x in source
            ]
            kept = lane < jnp.where(first, LANES - by[0], LANES - by[1])
            v[p].append([jnp.where(kept, turned[b], turned[b + 1]) for b in range(parts - 1)])
            phases_ref[p, 8 * q : 8 * q + 8, :] = jnp.concatenate(v[p][q], axis=1)
    count = parts - 2

    def window_sums(terms):
        wide = [
            jnp.concatenate(
                [
                    jnp.concatenate(
                        [jnp.concatenate([term[q][j + i] for i in range(2)], axis=1) for q in range(groups)], axis=0
                    ).astype(jnp.bfloat16)
                    for j in range(count)
                ],
                axis=0,
            )
            for term in terms
        ]
        band = jnp.concatenate([band_ref[...]] * len(terms), axis=0)
        return jnp.dot(jnp.concatenate(wide, axis=1), band, preferred_element_type=jnp.float32)

    square = [[[x * x for x in line] for line in v[p]] for p in range(S)]
    high = [[[x.astype(jnp.bfloat16).astype(jnp.float32) for x in line] for line in square[p]] for p in range(S)]
    low = [[[x - y for x, y in zip(a, b)] for a, b in zip(square[p], high[p])] for p in range(S)]
    sums = window_sums(v)
    powers = window_sums(high + low)
    for q in range(groups):
        weight = jnp.where(first, weights_ref[2 * q].astype(jnp.float32), weights_ref[2 * q + 1].astype(jnp.float32))
        for j in range(count):
            mean = sums[j * rows + 8 * q : j * rows + 8 * q + 8]
            power = powers[j * rows + 8 * q : j * rows + 8 * q + 8]
            for r in range(S):
                middle = mean * (1.0 / LENGTH)
                spread = power * (1.0 / LENGTH) - middle * middle
                factor_ref[r, 8 * q : 8 * q + 8, LANES * j : LANES * (j + 1)] = weight / (LENGTH * jnp.sqrt(spread + EPS))
                mean = mean + (v[0][q][j + 1] - v[0][q][j])
                power = power + (square[0][q][j + 1] - square[0][q][j])


def owner_sum(lags, precise, step, sides, away, restore_ref, wide_ref, last_ref, phases_ref, factor_ref, out_ref, sum_ref):
    pairs, _, count, _ = wide_ref.shape
    stations = phases_ref.shape[1] // SLOTS
    side, core = lax.rem(lax.axis_index("sta") + step, sides), lax.axis_index("comp")
    owner = 2 * side + (1 - core if away else core)
    lane = iota((8, LANES), 1)
    sub = iota((8, LANES), 0)
    width = lags // S
    for n in range(width // TILE):
        begin = pl.multiple_of(owner * width + n * TILE, LANES)
        extra = phases_ref[0, :, pl.ds(begin + LANES, TILE)] * factor_ref[1, :, pl.ds(begin, TILE)]
        extra = jnp.concatenate([extra, jnp.zeros((LANES - SLOTS * stations, TILE), jnp.float32)], axis=0).astype(jnp.bfloat16)
        past = jnp.dot(last_ref[...], extra, preferred_element_type=jnp.float32)
        for pair in range(pairs):
            slot = SLOTS * (pair % stations) + pair // stations
            rows = []
            for p in range(S):
                line = [
                    jnp.broadcast_to(phases_ref[p, slot : slot + 1, pl.ds(begin + LANES * j, LANES)], (8, LANES))
                    for j in range(3)
                ]
                for g in range(0, LANES, 16):
                    sides_of = []
                    for j in range(2):
                        pieces = []
                        for h in (g, g + 8):
                            mixed = jnp.where(lane >= LANES - 1 - h - sub, line[j], line[j + 1])
                            pieces.append(pltpu.roll(mixed, 1 + h, axis=1, stride=1, stride_axis=0))
                        sides_of.append(jnp.concatenate(pieces, axis=0).astype(jnp.bfloat16))
                    rows.append(jnp.concatenate(sides_of, axis=1))
            table = jnp.concatenate(rows, axis=0)
            units = jnp.concatenate(
                [jnp.concatenate([wide_ref[pair, v] for v in PHASE_PIECES[r]], axis=1) for r in range(S)], axis=0
            )
            products = jnp.dot(units, table, preferred_element_type=jnp.float32)
            for r in range(S):
                scaled = products[r * count : (r + 1) * count] * factor_ref[r, slot : slot + 1, pl.ds(begin, TILE)]
                where = (slice(r * count, (r + 1) * count), slice(n * TILE, (n + 1) * TILE))
                if pair:
                    sum_ref[where] += scaled
                else:
                    sum_ref[where] = scaled + past if r == 1 else scaled
    total = jnp.concatenate([sum_ref[r * count : (r + 1) * count, :] for r in range(S)], axis=1)
    pieces = [total.astype(jnp.bfloat16)]
    if precise:
        pieces.append((total - pieces[0].astype(jnp.float32)).astype(jnp.bfloat16))
    moved = jnp.dot(jnp.concatenate(pieces, axis=0), restore_ref[...], preferred_element_type=jnp.float32)
    out_ref[...] = moved[:count] + moved[count:] if precise else moved.astype(jnp.bfloat16)


def first_kernel(blocks, static, offsets_ref, weights_ref, split_ref, band_ref, restore_ref, wide_ref, last_ref, *refs):
    block_refs = refs[: blocks + 1]
    phases_ref, factor_ref, out_ref, raw_ref, sum_ref = refs[blocks + 1 :]
    records(offsets_ref, weights_ref, split_ref, band_ref, block_refs, phases_ref, factor_ref, raw_ref)
    owner_sum(*static, restore_ref, wide_ref, last_ref, phases_ref, factor_ref, out_ref, sum_ref)


def later_kernel(static, *refs):
    owner_sum(*static, *refs)


def call_parts(static, wide):
    lags, precise = static[:2]
    pairs, _, count, _ = wide.shape
    shape = jax.ShapeDtypeStruct((count, lags), jnp.float32 if precise else jnp.bfloat16)
    scratch = pltpu.VMEM((S * count, lags // S), jnp.float32)
    params = dict(
        compiler_params=pltpu.CompilerParams(vmem_limit_bytes=16 << 20),
        cost_estimate=pl.CostEstimate(flops=2 * count * pairs * LENGTH * lags, bytes_accessed=4 * 10**6, transcendentals=0),
    )
    return shape, scratch, params


def first_sum(static, offsets, weights, split, band, restore, wide, last, blocks, tail):
    comps, stations, width = blocks[0].shape
    rows = SLOTS * stations
    parts = (len(blocks) * width + tail.shape[-1]) // LENGTH
    shape, scratch, params = call_parts(static, wide)
    return pl.pallas_call(
        functools.partial(first_kernel, len(blocks), static),
        out_shape=(
            jax.ShapeDtypeStruct((S, rows, (parts - 1) * LANES), jnp.float32),
            jax.ShapeDtypeStruct((S, rows, (parts - 2) * LANES), jnp.float32),
            shape,
        ),
        in_specs=[SMEM, SMEM] + [VMEM] * (6 + len(blocks)),
        out_specs=(VMEM,) * 3,
        scratch_shapes=[pltpu.VMEM((S * parts, rows, LANES), jnp.float32), scratch],
        name="records_sum",
        **params,
    )(offsets, weights, split, band, restore, wide, last, *blocks, tail)


def later_sum(static, restore, wide, last, tables):
    shape, scratch, params = call_parts(static, wide)
    return pl.pallas_call(
        functools.partial(later_kernel, static),
        out_shape=shape,
        in_specs=[VMEM] * 5,
        out_specs=VMEM,
        scratch_shapes=[scratch],
        name="sum",
        **params,
    )(restore, wide, last, *tables)


def pick_kernel(restore_ref, split_ref, order_ref, band_ref):
    lags = restore_ref.shape[0]
    width = lags // S
    row = iota((lags, 1), 0)
    restore_ref[...] = ones_where(iota((lags, lags), 1) == S * (row % width) + row // width)
    sample = iota((LENGTH, LENGTH), 0)
    column = iota((1, LENGTH), 1)
    split_ref[...] = ones_where(sample == S * (column % LANES) + column // LANES)
    order_ref[...] = ones_where(sample == S * (LANES - 1 - column % LANES) + column // LANES)
    ahead = iota((2 * LANES, LANES), 0) - iota((2 * LANES, LANES), 1)
    band_ref[...] = ones_where((ahead >= 0) & (ahead < LANES))


def picks(lags):
    return pl.pallas_call(
        pick_kernel,
        out_shape=tuple(
            jax.ShapeDtypeStruct(shape, jnp.bfloat16)
            for shape in ((lags, lags), (LENGTH, LENGTH), (LENGTH, LENGTH), (2 * LANES, LANES))
        ),
        out_specs=(VMEM,) * 4,
        compiler_params=pltpu.CompilerParams(vmem_limit_bytes=4 << 20),
        cost_estimate=pl.CostEstimate(flops=4 * 10**9, bytes_accessed=4096, transcendentals=0),
        name="picks",
    )()


def shards(templates, data, tail, offsets, weights, mask):
    owners = lax.axis_size("tmpl")
    sides = lax.axis_size("sta")
    lags = owners * data.shape[-1] // (2 * sides)
    block = jnp.transpose(data, (1, 0, 2))
    closing = jnp.transpose(tail, (1, 0, 2))
    restore, split, order, band = picks(lags)
    if owners <= 4:
        blocks = [block] + [
            lax.ppermute(block, "tmpl", [(i, (i - d) % owners) for i in range(owners)]) for d in range(1, owners)
        ]
    else:
        gathered = lax.all_gather(block, "tmpl", axis=0, tiled=False)
        place = lax.axis_index("tmpl")
        blocks = [lax.dynamic_index_in_dim(gathered, lax.rem(place + d, owners), 0, False) for d in range(owners)]
    wide, last = templates_prepared(templates, mask, order)
    gotten = []
    for d in range(1, sides + 1):
        precise = d == sides
        if d == 1:
            *tables, away = first_sum((lags, False, d, sides, True), offsets, weights, split, band, restore, wide, last, blocks, closing)
        else:
            held, _ = lax.optimization_barrier((last, both))
            away = later_sum((lags, False, d, sides, True), restore, wide, held, tables)
        got = lax.ppermute(away, "comp", [(0, 1), (1, 0)])
        held, _ = lax.optimization_barrier((last, away))
        keep = later_sum((lags, precise, d, sides, False), restore, wide, held, tables)
        if d < sides:
            both = (keep.astype(jnp.float32) + got.astype(jnp.float32)).astype(jnp.bfloat16)
            gotten.append(lax.ppermute(both, "sta", [(i, (i + d) % sides) for i in range(sides)]))
    total = keep
    for term in gotten:
        total = total + term.astype(jnp.float32)
    if gotten:
        total = lax.optimization_barrier(total)
    return total + got.astype(jnp.float32)


def solution(mesh):
    in_specs = (
        P(("groups", "tmpl"), ("sta", "comp"), None, None),
        P(("groups", "sta", "comp"), None, "tmpl"),
        P(("groups", "sta", "comp"), None, None),
        P(("groups", "sta", "comp")),
        P(("groups", "sta", "comp")),
        P(("groups", "tmpl"), ("sta", "comp")),
    )
    out_specs = P(("groups", "tmpl"), ("sta", "comp"))
    return jax.shard_map(shards, mesh=mesh, in_specs=in_specs, out_specs=out_specs, check_vma=False)
```

```python
import functools

import jax
import jax.numpy as jnp
from jax import lax
from jax.experimental import pallas as pl
from jax.experimental.pallas import tpu as pltpu
from jax.sharding import PartitionSpec as P

EPS = 1e-05
SLOTS = 4
S = 2
LANES = 128
LENGTH = S * LANES
TILE = 2 * LANES
VMEM = pl.BlockSpec(memory_space=pltpu.VMEM)
SMEM = pl.BlockSpec(memory_space=pltpu.SMEM)
PHASE_PIECES = ((0, 1), (2, 0))


def iota(shape, axis):
    return lax.broadcasted_iota(jnp.int32, shape, axis)


def ones_where(condition):
    return jnp.where(condition, 1.0, 0.0).astype(jnp.bfloat16)


def later(x, by):
    return pltpu.roll(x, x.shape[-1] - by, axis=1)


def template_kernel(x_ref, mask_ref, order_ref, wide_ref, last_ref, unit_ref, rows_ref):
    count, comps, stations, length = x_ref.shape
    pairs = comps * stations
    pitch = unit_ref.shape[1] // count
    group = min(8, count)
    lane = iota((count, LANES), 1)
    last = jnp.zeros((count, LANES), jnp.float32)
    available = jnp.transpose(mask_ref[...].astype(jnp.float32))
    for at in range(0, count, group):
        values = x_ref[at : at + group].astype(jnp.float32).reshape(group * pairs, length)
        centred = values - jnp.sum(values, axis=-1, keepdims=True) * (1.0 / length)
        spread = jnp.sum(centred * centred, axis=-1, keepdims=True) * (1.0 / length)
        unit = centred * lax.rsqrt(spread + EPS)
        for h in range(length // LANES):
            for t in range(group):
                unit_ref[h, (at + t) * pitch : (at + t) * pitch + pairs, :] = unit[t * pairs : (t + 1) * pairs, LANES * h : LANES * (h + 1)]
    for s in range(stations):
        column = available[:, s : s + 1]
        for c in range(comps):
            pair = c * stations + s
            rows = jnp.concatenate(
                [unit_ref[h, pl.ds(pair, count, stride=pitch), :] for h in range(length // LANES)], axis=1
            )
            rows_ref[pair * count : (pair + 1) * count, :] = (rows * column).astype(jnp.bfloat16)
    batch = 3
    for at in range(0, pairs, batch):
        moved = jnp.dot(rows_ref[at * count : (at + batch) * count, :], order_ref[...], preferred_element_type=jnp.float32)
        for i in range(batch):
            pair = at + i
            even = moved[i * count : (i + 1) * count, :LANES]
            odd = moved[i * count : (i + 1) * count, LANES:]
            wide_ref[pair, 0] = even.astype(jnp.bfloat16)
            wide_ref[pair, 1] = odd.astype(jnp.bfloat16)
            wide_ref[pair, 2] = jnp.where(lane == LANES - 1, 0.0, later(odd, 1)).astype(jnp.bfloat16)
            slot = SLOTS * (pair % stations) + pair // stations
            last = jnp.where(lane == slot, pltpu.roll(odd, slot, axis=1), last)
    last_ref[...] = last.astype(jnp.bfloat16)


def templates_prepared(templates, mask, order):
    count, stations, comps, length = templates.shape
    pairs = stations * comps
    return pl.pallas_call(
        template_kernel,
        out_shape=(
            jax.ShapeDtypeStruct((pairs, 3, count, LANES), jnp.bfloat16),
            jax.ShapeDtypeStruct((count, LANES), jnp.bfloat16),
        ),
        in_specs=[VMEM, VMEM, VMEM],
        out_specs=(VMEM, VMEM),
        scratch_shapes=[
            pltpu.VMEM((length // LANES, (pairs + 1) * count, LANES), jnp.float32),
            pltpu.VMEM((pairs * count, length), jnp.bfloat16),
        ],
        compiler_params=pltpu.CompilerParams(vmem_limit_bytes=16 << 20),
        cost_estimate=pl.CostEstimate(flops=2 * 10**9, bytes_accessed=8 * 10**6, transcendentals=0),
        name="templates",
    )(jnp.transpose(templates, (0, 2, 1, 3)), jnp.transpose(mask), order)


def records(offsets_ref, weights_ref, split_ref, band_ref, block_refs, phases_ref, factor_ref, raw_ref):
    blocks = len(block_refs) - 1
    comps, stations, width = block_refs[0].shape
    rows = stations * SLOTS
    per = width // LENGTH
    for i in range(blocks + 1):
        home = blocks if i == blocks else lax.rem(lax.axis_index("tmpl") + i, blocks)
        for j in range(block_refs[i].shape[-1] // LANES):
            for c in range(SLOTS):
                if c < comps:
                    values = block_refs[i][c, :, LANES * j : LANES * (j + 1)].astype(jnp.float32)
                else:
                    values = jnp.zeros((stations, LANES), jnp.float32)
                raw_ref[home * per * S + j, pl.ds(c, stations, stride=SLOTS), :] = values
    parts = raw_ref.shape[0] // S
    flat = jnp.concatenate(
        [jnp.concatenate([raw_ref[S * b + i] for i in range(S)], axis=1) for b in range(parts)], axis=0
    ).astype(jnp.bfloat16)
    split = jnp.dot(flat, split_ref[...], preferred_element_type=jnp.float32)
    lane = iota((8, LANES), 1)
    first = iota((8, LANES), 0) < SLOTS
    groups = rows // 8
    v = [[], []]
    for q in range(groups):
        offset = [offsets_ref[2 * q], offsets_ref[2 * q + 1]]
        odd = jnp.where(first, offset[0] & 1, offset[1] & 1) != 0
        held = [[split[b * rows + 8 * q : b * rows + 8 * q + 8, LANES * p : LANES * (p + 1)] for b in range(parts)] for p in range(S)]
        for p in range(S):
            source = [jnp.where(odd, held[1 - p][b], held[p][b]) for b in range(parts)]
            by = [(o + p) // S for o in offset]
            turned = [
                jnp.where(first, pltpu.roll(x, (LANES - by[0]) % LANES, axis=1), pltpu.roll(x, (LANES - by[1]) % LANES, axis=1))
                for x in source
            ]
            kept = lane < jnp.where(first, LANES - by[0], LANES - by[1])
            v[p].append([jnp.where(kept, turned[b], turned[b + 1]) for b in range(parts - 1)])
            phases_ref[p, 8 * q : 8 * q + 8, :] = jnp.concatenate(v[p][q], axis=1)
    count = parts - 2

    def window_sums(terms):
        wide = [
            jnp.concatenate(
                [
                    jnp.concatenate(
                        [jnp.concatenate([term[q][j + i] for i in range(2)], axis=1) for q in range(groups)], axis=0
                    ).astype(jnp.bfloat16)
                    for j in range(count)
                ],
                axis=0,
            )
            for term in terms
        ]
        band = jnp.concatenate([band_ref[...]] * len(terms), axis=0)
        return jnp.dot(jnp.concatenate(wide, axis=1), band, preferred_element_type=jnp.float32)

    square = [[[x * x for x in line] for line in v[p]] for p in range(S)]
    high = [[[x.astype(jnp.bfloat16).astype(jnp.float32) for x in line] for line in square[p]] for p in range(S)]
    low = [[[x - y for x, y in zip(a, b)] for a, b in zip(square[p], high[p])] for p in range(S)]
    sums = window_sums(v)
    powers = window_sums(high + low)
    for q in range(groups):
        weight = jnp.where(first, weights_ref[2 * q].astype(jnp.float32), weights_ref[2 * q + 1].astype(jnp.float32))
        for j in range(count):
            mean = sums[j * rows + 8 * q : j * rows + 8 * q + 8]
            power = powers[j * rows + 8 * q : j * rows + 8 * q + 8]
            for r in range(S):
                middle = mean * (1.0 / LENGTH)
                spread = power * (1.0 / LENGTH) - middle * middle
                factor_ref[r, 8 * q : 8 * q + 8, LANES * j : LANES * (j + 1)] = weight / (LENGTH * jnp.sqrt(spread + EPS))
                mean = mean + (v[0][q][j + 1] - v[0][q][j])
                power = power + (square[0][q][j + 1] - square[0][q][j])


def owner_sum(lags, precise, step, sides, away, restore_ref, wide_ref, last_ref, phases_ref, factor_ref, out_ref, sum_ref):
    pairs, _, count, _ = wide_ref.shape
    stations = phases_ref.shape[1] // SLOTS
    side, core = lax.rem(lax.axis_index("sta") + step, sides), lax.axis_index("comp")
    owner = 2 * side + (1 - core if away else core)
    lane = iota((8, LANES), 1)
    sub = iota((8, LANES), 0)
    width = lags // S
    for n in range(width // TILE):
        begin = pl.multiple_of(owner * width + n * TILE, LANES)
        extra = phases_ref[0, :, pl.ds(begin + LANES, TILE)] * factor_ref[1, :, pl.ds(begin, TILE)]
        extra = jnp.concatenate([extra, jnp.zeros((LANES - SLOTS * stations, TILE), jnp.float32)], axis=0).astype(jnp.bfloat16)
        past = jnp.dot(last_ref[...], extra, preferred_element_type=jnp.float32)
        for pair in range(pairs):
            slot = SLOTS * (pair % stations) + pair // stations
            rows = []
            for p in range(S):
                line = [
                    jnp.broadcast_to(phases_ref[p, slot : slot + 1, pl.ds(begin + LANES * j, LANES)], (8, LANES))
                    for j in range(3)
                ]
                for g in range(0, LANES, 16):
                    sides_of = []
                    for j in range(2):
                        pieces = []
                        for h in (g, g + 8):
                            mixed = jnp.where(lane >= LANES - 1 - h - sub, line[j], line[j + 1])
                            pieces.append(pltpu.roll(mixed, 1 + h, axis=1, stride=1, stride_axis=0))
                        sides_of.append(jnp.concatenate(pieces, axis=0).astype(jnp.bfloat16))
                    rows.append(jnp.concatenate(sides_of, axis=1))
            table = jnp.concatenate(rows, axis=0)
            units = jnp.concatenate(
                [jnp.concatenate([wide_ref[pair, v] for v in PHASE_PIECES[r]], axis=1) for r in range(S)], axis=0
            )
            products = jnp.dot(units, table, preferred_element_type=jnp.float32)
            for r in range(S):
                scaled = products[r * count : (r + 1) * count] * factor_ref[r, slot : slot + 1, pl.ds(begin, TILE)]
                where = (slice(r * count, (r + 1) * count), slice(n * TILE, (n + 1) * TILE))
                if pair:
                    sum_ref[where] += scaled
                else:
                    sum_ref[where] = scaled + past if r == 1 else scaled
    total = jnp.concatenate([sum_ref[r * count : (r + 1) * count, :] for r in range(S)], axis=1)
    pieces = [total.astype(jnp.bfloat16)]
    if precise:
        pieces.append((total - pieces[0].astype(jnp.float32)).astype(jnp.bfloat16))
    moved = jnp.dot(jnp.concatenate(pieces, axis=0), restore_ref[...], preferred_element_type=jnp.float32)
    out_ref[...] = moved[:count] + moved[count:] if precise else moved.astype(jnp.bfloat16)


def first_kernel(blocks, static, offsets_ref, weights_ref, split_ref, band_ref, restore_ref, wide_ref, last_ref, *refs):
    block_refs = refs[: blocks + 1]
    phases_ref, factor_ref, out_ref, raw_ref, sum_ref = refs[blocks + 1 :]
    records(offsets_ref, weights_ref, split_ref, band_ref, block_refs, phases_ref, factor_ref, raw_ref)
    owner_sum(*static, restore_ref, wide_ref, last_ref, phases_ref, factor_ref, out_ref, sum_ref)


def later_kernel(static, *refs):
    owner_sum(*static, *refs)


def call_parts(static, wide):
    lags, precise = static[:2]
    pairs, _, count, _ = wide.shape
    shape = jax.ShapeDtypeStruct((count, lags), jnp.float32 if precise else jnp.bfloat16)
    scratch = pltpu.VMEM((S * count, lags // S), jnp.float32)
    params = dict(
        compiler_params=pltpu.CompilerParams(vmem_limit_bytes=16 << 20),
        cost_estimate=pl.CostEstimate(flops=2 * count * pairs * LENGTH * lags, bytes_accessed=4 * 10**6, transcendentals=0),
    )
    return shape, scratch, params


def first_sum(static, offsets, weights, split, band, restore, wide, last, blocks, tail):
    comps, stations, width = blocks[0].shape
    rows = SLOTS * stations
    parts = (len(blocks) * width + tail.shape[-1]) // LENGTH
    shape, scratch, params = call_parts(static, wide)
    return pl.pallas_call(
        functools.partial(first_kernel, len(blocks), static),
        out_shape=(
            jax.ShapeDtypeStruct((S, rows, (parts - 1) * LANES), jnp.float32),
            jax.ShapeDtypeStruct((S, rows, (parts - 2) * LANES), jnp.float32),
            shape,
        ),
        in_specs=[SMEM, SMEM] + [VMEM] * (6 + len(blocks)),
        out_specs=(VMEM,) * 3,
        scratch_shapes=[pltpu.VMEM((S * parts, rows, LANES), jnp.float32), scratch],
        name="records_sum",
        **params,
    )(offsets, weights, split, band, restore, wide, last, *blocks, tail)


def later_sum(static, restore, wide, last, tables):
    shape, scratch, params = call_parts(static, wide)
    return pl.pallas_call(
        functools.partial(later_kernel, static),
        out_shape=shape,
        in_specs=[VMEM] * 5,
        out_specs=VMEM,
        scratch_shapes=[scratch],
        name="sum",
        **params,
    )(restore, wide, last, *tables)


def pick_kernel(restore_ref, split_ref, order_ref, band_ref):
    lags = restore_ref.shape[0]
    width = lags // S
    row = iota((lags, 1), 0)
    restore_ref[...] = ones_where(iota((lags, lags), 1) == S * (row % width) + row // width)
    sample = iota((LENGTH, LENGTH), 0)
    column = iota((1, LENGTH), 1)
    split_ref[...] = ones_where(sample == S * (column % LANES) + column // LANES)
    order_ref[...] = ones_where(sample == S * (LANES - 1 - column % LANES) + column // LANES)
    ahead = iota((2 * LANES, LANES), 0) - iota((2 * LANES, LANES), 1)
    band_ref[...] = ones_where((ahead >= 0) & (ahead < LANES))


def picks(lags):
    return pl.pallas_call(
        pick_kernel,
        out_shape=tuple(
            jax.ShapeDtypeStruct(shape, jnp.bfloat16)
            for shape in ((lags, lags), (LENGTH, LENGTH), (LENGTH, LENGTH), (2 * LANES, LANES))
        ),
        out_specs=(VMEM,) * 4,
        compiler_params=pltpu.CompilerParams(vmem_limit_bytes=4 << 20),
        cost_estimate=pl.CostEstimate(flops=4 * 10**9, bytes_accessed=4096, transcendentals=0),
        name="picks",
    )()


def shards(templates, data, tail, offsets, weights, mask):
    owners = lax.axis_size("tmpl")
    sides = lax.axis_size("sta")
    lags = owners * data.shape[-1] // (2 * sides)
    block = jnp.transpose(data, (1, 0, 2))
    closing = jnp.transpose(tail, (1, 0, 2))
    restore, split, order, band = picks(lags)
    if owners <= 4:
        blocks = [block] + [
            lax.ppermute(block, "tmpl", [(i, (i - d) % owners) for i in range(owners)]) for d in range(1, owners)
        ]
    else:
        gathered = lax.all_gather(block, "tmpl", axis=0, tiled=False)
        place = lax.axis_index("tmpl")
        blocks = [lax.dynamic_index_in_dim(gathered, lax.rem(place + d, owners), 0, False) for d in range(owners)]
    wide, last = templates_prepared(templates, mask, order)
    gotten = []
    for d in range(1, sides + 1):
        precise = d == sides
        if d == 1:
            *tables, away = first_sum((lags, False, d, sides, True), offsets, weights, split, band, restore, wide, last, blocks, closing)
        else:
            held, _ = lax.optimization_barrier((last, both))
            away = later_sum((lags, False, d, sides, True), restore, wide, held, tables)
        got = lax.ppermute(away, "comp", [(0, 1), (1, 0)])
        held, _ = lax.optimization_barrier((last, away))
        keep = later_sum((lags, precise, d, sides, False), restore, wide, held, tables)
        if d < sides:
            both = (keep.astype(jnp.float32) + got.astype(jnp.float32)).astype(jnp.bfloat16)
            gotten.append(lax.ppermute(both, "sta", [(i, (i + d) % sides) for i in range(sides)]))
    total = keep
    for term in gotten:
        total = total + term.astype(jnp.float32)
    if gotten:
        total = lax.optimization_barrier(total)
    return total + got.astype(jnp.float32)


def solution(mesh):
    in_specs = (
        P(("groups", "tmpl"), ("sta", "comp"), None, None),
        P(("groups", "sta", "comp"), None, "tmpl"),
        P(("groups", "sta", "comp"), None, None),
        P(("groups", "sta", "comp")),
        P(("groups", "sta", "comp")),
        P(("groups", "tmpl"), ("sta", "comp")),
    )
    out_specs = P(("groups", "tmpl"), ("sta", "comp"))
    return jax.shard_map(shards, mesh=mesh, in_specs=in_specs, out_specs=out_specs, check_vma=False)
```

```python
import functools

import jax
import jax.numpy as jnp
from jax import lax
from jax.experimental import pallas as pl
from jax.experimental.pallas import tpu as pltpu
from jax.sharding import PartitionSpec as P

EPS = 1e-05
SLOTS = 4
S = 2
LANES = 128
LENGTH = S * LANES
TILE = 2 * LANES
VMEM = pl.BlockSpec(memory_space=pltpu.VMEM)
SMEM = pl.BlockSpec(memory_space=pltpu.SMEM)
PHASE_PIECES = ((0, 1), (2, 0))


def iota(shape, axis):
    return lax.broadcasted_iota(jnp.int32, shape, axis)


def ones_where(condition):
    return jnp.where(condition, 1.0, 0.0).astype(jnp.bfloat16)


def later(x, by):
    return pltpu.roll(x, x.shape[-1] - by, axis=1)


def template_kernel(x_ref, mask_ref, order_ref, wide_ref, last_ref, unit_ref, rows_ref):
    count, comps, stations, length = x_ref.shape
    pairs = comps * stations
    pitch = unit_ref.shape[1] // count
    group = min(8, count)
    lane = iota((count, LANES), 1)
    last = jnp.zeros((count, LANES), jnp.float32)
    available = jnp.transpose(mask_ref[...].astype(jnp.float32))
    for at in range(0, count, group):
        values = x_ref[at : at + group].astype(jnp.float32).reshape(group * pairs, length)
        centred = values - jnp.sum(values, axis=-1, keepdims=True) * (1.0 / length)
        spread = jnp.sum(centred * centred, axis=-1, keepdims=True) * (1.0 / length)
        unit = centred * lax.rsqrt(spread + EPS)
        for h in range(length // LANES):
            for t in range(group):
                unit_ref[h, (at + t) * pitch : (at + t) * pitch + pairs, :] = unit[t * pairs : (t + 1) * pairs, LANES * h : LANES * (h + 1)]
    for s in range(stations):
        column = available[:, s : s + 1]
        for c in range(comps):
            pair = c * stations + s
            rows = jnp.concatenate(
                [unit_ref[h, pl.ds(pair, count, stride=pitch), :] for h in range(length // LANES)], axis=1
            )
            rows_ref[pair * count : (pair + 1) * count, :] = (rows * column).astype(jnp.bfloat16)
    batch = 2
    for at in range(0, pairs, batch):
        moved = jnp.dot(rows_ref[at * count : (at + batch) * count, :], order_ref[...], preferred_element_type=jnp.float32)
        for i in range(batch):
            pair = at + i
            even = moved[i * count : (i + 1) * count, :LANES]
            odd = moved[i * count : (i + 1) * count, LANES:]
            wide_ref[pair, 0] = even.astype(jnp.bfloat16)
            wide_ref[pair, 1] = odd.astype(jnp.bfloat16)
            wide_ref[pair, 2] = jnp.where(lane == LANES - 1, 0.0, later(odd, 1)).astype(jnp.bfloat16)
            slot = SLOTS * (pair % stations) + pair // stations
            last = jnp.where(lane == slot, pltpu.roll(odd, slot, axis=1), last)
    last_ref[...] = last.astype(jnp.bfloat16)


def templates_prepared(templates, mask, order):
    count, stations, comps, length = templates.shape
    pairs = stations * comps
    return pl.pallas_call(
        template_kernel,
        out_shape=(
            jax.ShapeDtypeStruct((pairs, 3, count, LANES), jnp.bfloat16),
            jax.ShapeDtypeStruct((count, LANES), jnp.bfloat16),
        ),
        in_specs=[VMEM, VMEM, VMEM],
        out_specs=(VMEM, VMEM),
        scratch_shapes=[
            pltpu.VMEM((length // LANES, (pairs + 1) * count, LANES), jnp.float32),
            pltpu.VMEM((pairs * count, length), jnp.bfloat16),
        ],
        compiler_params=pltpu.CompilerParams(vmem_limit_bytes=16 << 20),
        cost_estimate=pl.CostEstimate(flops=2 * 10**9, bytes_accessed=8 * 10**6, transcendentals=0),
        name="templates",
    )(jnp.transpose(templates, (0, 2, 1, 3)), jnp.transpose(mask), order)


def records(offsets_ref, weights_ref, split_ref, band_ref, block_refs, phases_ref, factor_ref, raw_ref):
    blocks = len(block_refs) - 1
    comps, stations, width = block_refs[0].shape
    rows = stations * SLOTS
    per = width // LENGTH
    for i in range(blocks + 1):
        home = blocks if i == blocks else lax.rem(lax.axis_index("tmpl") + i, blocks)
        for j in range(block_refs[i].shape[-1] // LANES):
            for c in range(SLOTS):
                if c < comps:
                    values = block_refs[i][c, :, LANES * j : LANES * (j + 1)].astype(jnp.float32)
                else:
                    values = jnp.zeros((stations, LANES), jnp.float32)
                raw_ref[home * per * S + j, pl.ds(c, stations, stride=SLOTS), :] = values
    parts = raw_ref.shape[0] // S
    flat = jnp.concatenate(
        [jnp.concatenate([raw_ref[S * b + i] for i in range(S)], axis=1) for b in range(parts)], axis=0
    ).astype(jnp.bfloat16)
    split = jnp.dot(flat, split_ref[...], preferred_element_type=jnp.float32)
    lane = iota((8, LANES), 1)
    first = iota((8, LANES), 0) < SLOTS
    groups = rows // 8
    v = [[], []]
    for q in range(groups):
        offset = [offsets_ref[2 * q], offsets_ref[2 * q + 1]]
        odd = jnp.where(first, offset[0] & 1, offset[1] & 1) != 0
        held = [[split[b * rows + 8 * q : b * rows + 8 * q + 8, LANES * p : LANES * (p + 1)] for b in range(parts)] for p in range(S)]
        for p in range(S):
            source = [jnp.where(odd, held[1 - p][b], held[p][b]) for b in range(parts)]
            by = [(o + p) // S for o in offset]
            turned = [
                jnp.where(first, pltpu.roll(x, (LANES - by[0]) % LANES, axis=1), pltpu.roll(x, (LANES - by[1]) % LANES, axis=1))
                for x in source
            ]
            kept = lane < jnp.where(first, LANES - by[0], LANES - by[1])
            v[p].append([jnp.where(kept, turned[b], turned[b + 1]) for b in range(parts - 1)])
            phases_ref[p, 8 * q : 8 * q + 8, :] = jnp.concatenate(v[p][q], axis=1)
    count = parts - 2

    def window_sums(terms):
        wide = [
            jnp.concatenate(
                [
                    jnp.concatenate(
                        [jnp.concatenate([term[q][j + i] for i in range(2)], axis=1) for q in range(groups)], axis=0
                    ).astype(jnp.bfloat16)
                    for j in range(count)
                ],
                axis=0,
            )
            for term in terms
        ]
        band = jnp.concatenate([band_ref[...]] * len(terms), axis=0)
        return jnp.dot(jnp.concatenate(wide, axis=1), band, preferred_element_type=jnp.float32)

    square = [[[x * x for x in line] for line in v[p]] for p in range(S)]
    high = [[[x.astype(jnp.bfloat16).astype(jnp.float32) for x in line] for line in square[p]] for p in range(S)]
    low = [[[x - y for x, y in zip(a, b)] for a, b in zip(square[p], high[p])] for p in range(S)]
    sums = window_sums(v)
    powers = window_sums(high + low)
    for q in range(groups):
        weight = jnp.where(first, weights_ref[2 * q].astype(jnp.float32), weights_ref[2 * q + 1].astype(jnp.float32))
        for j in range(count):
            mean = sums[j * rows + 8 * q : j * rows + 8 * q + 8]
            power = powers[j * rows + 8 * q : j * rows + 8 * q + 8]
            for r in range(S):
                middle = mean * (1.0 / LENGTH)
                spread = power * (1.0 / LENGTH) - middle * middle
                factor_ref[r, 8 * q : 8 * q + 8, LANES * j : LANES * (j + 1)] = weight / (LENGTH * jnp.sqrt(spread + EPS))
                mean = mean + (v[0][q][j + 1] - v[0][q][j])
                power = power + (square[0][q][j + 1] - square[0][q][j])


def owner_sum(lags, precise, step, sides, away, restore_ref, wide_ref, last_ref, phases_ref, factor_ref, out_ref, sum_ref):
    pairs, _, count, _ = wide_ref.shape
    stations = phases_ref.shape[1] // SLOTS
    side, core = lax.rem(lax.axis_index("sta") + step, sides), lax.axis_index("comp")
    owner = 2 * side + (1 - core if away else core)
    lane = iota((8, LANES), 1)
    sub = iota((8, LANES), 0)
    width = lags // S
    for n in range(width // TILE):
        begin = pl.multiple_of(owner * width + n * TILE, LANES)
        extra = phases_ref[0, :, pl.ds(begin + LANES, TILE)] * factor_ref[1, :, pl.ds(begin, TILE)]
        extra = jnp.concatenate([extra, jnp.zeros((LANES - SLOTS * stations, TILE), jnp.float32)], axis=0).astype(jnp.bfloat16)
        past = jnp.dot(last_ref[...], extra, preferred_element_type=jnp.float32)
        for pair in range(pairs):
            slot = SLOTS * (pair % stations) + pair // stations
            rows = []
            for p in range(S):
                line = [
                    jnp.broadcast_to(phases_ref[p, slot : slot + 1, pl.ds(begin + LANES * j, LANES)], (8, LANES))
                    for j in range(3)
                ]
                for g in range(0, LANES, 16):
                    sides_of = []
                    for j in range(2):
                        pieces = []
                        for h in (g, g + 8):
                            mixed = jnp.where(lane >= LANES - 1 - h - sub, line[j], line[j + 1])
                            pieces.append(pltpu.roll(mixed, 1 + h, axis=1, stride=1, stride_axis=0))
                        sides_of.append(jnp.concatenate(pieces, axis=0).astype(jnp.bfloat16))
                    rows.append(jnp.concatenate(sides_of, axis=1))
            table = jnp.concatenate(rows, axis=0)
            units = jnp.concatenate(
                [jnp.concatenate([wide_ref[pair, v] for v in PHASE_PIECES[r]], axis=1) for r in range(S)], axis=0
            )
            products = jnp.dot(units, table, preferred_element_type=jnp.float32)
            for r in range(S):
                scaled = products[r * count : (r + 1) * count] * factor_ref[r, slot : slot + 1, pl.ds(begin, TILE)]
                where = (slice(r * count, (r + 1) * count), slice(n * TILE, (n + 1) * TILE))
                if pair:
                    sum_ref[where] += scaled
                else:
                    sum_ref[where] = scaled + past if r == 1 else scaled
    total = jnp.concatenate([sum_ref[r * count : (r + 1) * count, :] for r in range(S)], axis=1)
    pieces = [total.astype(jnp.bfloat16)]
    if precise:
        pieces.append((total - pieces[0].astype(jnp.float32)).astype(jnp.bfloat16))
    moved = jnp.dot(jnp.concatenate(pieces, axis=0), restore_ref[...], preferred_element_type=jnp.float32)
    out_ref[...] = moved[:count] + moved[count:] if precise else moved.astype(jnp.bfloat16)


def first_kernel(blocks, static, offsets_ref, weights_ref, split_ref, band_ref, restore_ref, wide_ref, last_ref, *refs):
    block_refs = refs[: blocks + 1]
    phases_ref, factor_ref, out_ref, raw_ref, sum_ref = refs[blocks + 1 :]
    records(offsets_ref, weights_ref, split_ref, band_ref, block_refs, phases_ref, factor_ref, raw_ref)
    owner_sum(*static, restore_ref, wide_ref, last_ref, phases_ref, factor_ref, out_ref, sum_ref)


def later_kernel(static, *refs):
    owner_sum(*static, *refs)


def call_parts(static, wide):
    lags, precise = static[:2]
    pairs, _, count, _ = wide.shape
    shape = jax.ShapeDtypeStruct((count, lags), jnp.float32 if precise else jnp.bfloat16)
    scratch = pltpu.VMEM((S * count, lags // S), jnp.float32)
    params = dict(
        compiler_params=pltpu.CompilerParams(vmem_limit_bytes=16 << 20),
        cost_estimate=pl.CostEstimate(flops=2 * count * pairs * LENGTH * lags, bytes_accessed=4 * 10**6, transcendentals=0),
    )
    return shape, scratch, params


def first_sum(static, offsets, weights, split, band, restore, wide, last, blocks, tail):
    comps, stations, width = blocks[0].shape
    rows = SLOTS * stations
    parts = (len(blocks) * width + tail.shape[-1]) // LENGTH
    shape, scratch, params = call_parts(static, wide)
    return pl.pallas_call(
        functools.partial(first_kernel, len(blocks), static),
        out_shape=(
            jax.ShapeDtypeStruct((S, rows, (parts - 1) * LANES), jnp.float32),
            jax.ShapeDtypeStruct((S, rows, (parts - 2) * LANES), jnp.float32),
            shape,
        ),
        in_specs=[SMEM, SMEM] + [VMEM] * (6 + len(blocks)),
        out_specs=(VMEM,) * 3,
        scratch_shapes=[pltpu.VMEM((S * parts, rows, LANES), jnp.float32), scratch],
        name="records_sum",
        **params,
    )(offsets, weights, split, band, restore, wide, last, *blocks, tail)


def later_sum(static, restore, wide, last, tables):
    shape, scratch, params = call_parts(static, wide)
    return pl.pallas_call(
        functools.partial(later_kernel, static),
        out_shape=shape,
        in_specs=[VMEM] * 5,
        out_specs=VMEM,
        scratch_shapes=[scratch],
        name="sum",
        **params,
    )(restore, wide, last, *tables)


def pick_kernel(restore_ref, split_ref, order_ref, band_ref):
    lags = restore_ref.shape[0]
    width = lags // S
    row = iota((lags, 1), 0)
    restore_ref[...] = ones_where(iota((lags, lags), 1) == S * (row % width) + row // width)
    sample = iota((LENGTH, LENGTH), 0)
    column = iota((1, LENGTH), 1)
    split_ref[...] = ones_where(sample == S * (column % LANES) + column // LANES)
    order_ref[...] = ones_where(sample == S * (LANES - 1 - column % LANES) + column // LANES)
    ahead = iota((2 * LANES, LANES), 0) - iota((2 * LANES, LANES), 1)
    band_ref[...] = ones_where((ahead >= 0) & (ahead < LANES))


def picks(lags):
    return pl.pallas_call(
        pick_kernel,
        out_shape=tuple(
            jax.ShapeDtypeStruct(shape, jnp.bfloat16)
            for shape in ((lags, lags), (LENGTH, LENGTH), (LENGTH, LENGTH), (2 * LANES, LANES))
        ),
        out_specs=(VMEM,) * 4,
        compiler_params=pltpu.CompilerParams(vmem_limit_bytes=4 << 20),
        cost_estimate=pl.CostEstimate(flops=4 * 10**9, bytes_accessed=4096, transcendentals=0),
        name="picks",
    )()


def shards(templates, data, tail, offsets, weights, mask):
    owners = lax.axis_size("tmpl")
    sides = lax.axis_size("sta")
    lags = owners * data.shape[-1] // (2 * sides)
    block = jnp.transpose(data, (1, 0, 2))
    closing = jnp.transpose(tail, (1, 0, 2))
    restore, split, order, band = picks(lags)
    if owners <= 4:
        blocks = [block] + [
            lax.ppermute(block, "tmpl", [(i, (i - d) % owners) for i in range(owners)]) for d in range(1, owners)
        ]
    else:
        gathered = lax.all_gather(block, "tmpl", axis=0, tiled=False)
        place = lax.axis_index("tmpl")
        blocks = [lax.dynamic_index_in_dim(gathered, lax.rem(place + d, owners), 0, False) for d in range(owners)]
    wide, last = templates_prepared(templates, mask, order)
    gotten = []
    for d in range(1, sides + 1):
        precise = d == sides
        if d == 1:
            *tables, away = first_sum((lags, False, d, sides, True), offsets, weights, split, band, restore, wide, last, blocks, closing)
        else:
            held, _ = lax.optimization_barrier((last, both))
            away = later_sum((lags, False, d, sides, True), restore, wide, held, tables)
        got = lax.ppermute(away, "comp", [(0, 1), (1, 0)])
        held, _ = lax.optimization_barrier((last, away))
        keep = later_sum((lags, precise, d, sides, False), restore, wide, held, tables)
        if d < sides:
            both = (keep.astype(jnp.float32) + got.astype(jnp.float32)).astype(jnp.bfloat16)
            gotten.append(lax.ppermute(both, "sta", [(i, (i + d) % sides) for i in range(sides)]))
    total = keep
    for term in gotten:
        total = total + term.astype(jnp.float32)
    if gotten:
        total = lax.optimization_barrier(total)
    return total + got.astype(jnp.float32)


def solution(mesh):
    in_specs = (
        P(("groups", "tmpl"), ("sta", "comp"), None, None),
        P(("groups", "sta", "comp"), None, "tmpl"),
        P(("groups", "sta", "comp"), None, None),
        P(("groups", "sta", "comp")),
        P(("groups", "sta", "comp")),
        P(("groups", "tmpl"), ("sta", "comp")),
    )
    out_specs = P(("groups", "tmpl"), ("sta", "comp"))
    return jax.shard_map(shards, mesh=mesh, in_specs=in_specs, out_specs=out_specs, check_vma=False)
```
